1024 devices in a mesh: replica: 32 (over y, x_hi, core), tensor: 32 (over z, x_lo).
Axes of the slice: x: 8 (x_hi: 2, x_lo: 4; x = x_hi * 4 + x_lo), y: 8, z: 8, core: 2. Of those that a mesh axis runs over, the one named last changes fastest.
Arguments:
- attn_out: bfloat16 [32, 768, 4096], P('replica', None, 'tensor'), may hold values from -6 to 6
- proj: bfloat16 [32, 4096, 2048], P('replica', 'tensor'), may hold values from -6 to 6
- momentum: bfloat16 [32, 4096, 2048], P('replica', 'tensor'), may hold values from -6 to 6
- target: bfloat16 [32, 768, 2048], P('replica'), may hold values from -6 to 6
- segment_ids: int32 [32, 768], P('replica'), may hold values from 0 to 95, never falling along the last dimension, each value on 1 to 192 neighbouring positions
- step: int32 [1], replicated, may hold values from 0 to 999
Outputs:
- projected: bfloat16 [32, 768, 2048], P('replica', 'tensor')
- attn_grad: bfloat16 [32, 768, 4096], P('replica', None, 'tensor')
- new_proj: bfloat16 [32, 4096, 2048], P('replica', 'tensor')
- new_moment: bfloat16 [32, 4096, 2048], P('replica', 'tensor')
The draws below stay inside these ranges and needn't reach their ends.
All inputs are finite; a program needn't handle non-finite values.
Results may differ from the reference program's by a relative error of at most 0.0055.
Values may be sent and summed in bfloat16 or wider, within the bound.
No kernel may reach another device: no remote copies, remote signals or barrier semaphores. Data moves between devices by JAX's collectives and lax.ppermute only.
A program may use at most 64 MiB of HBM per device.

```python
import math
import jax
import jax.numpy as jnp
import numpy as np
from jax import lax

HD = 128
HEADS_DEV = 1
DW = 2048
TOK = 768
HEADS = 32
SEGS = 96
SEG_MOST = 192
N_REPLICA = 32
N_TENSOR = 32


def block_levels(own_key, dims, shards, low, largest):
    def one(dim, blocks):
        draws = jax.random.uniform(jax.random.fold_in(jax.random.fold_in(own_key, 6), dim), (blocks,), jnp.float32, low / len(shards), largest / len(shards))
        return jnp.repeat(jnp.exp(draws), dims[dim] // blocks).reshape((-1,) + (1,) * (len(dims) - dim - 1))

    factor_of = one(*shards[0])
    for cut in shards[1:]:
        factor_of = factor_of * one(*cut)
    return factor_of


def length_profile(amount, total, bound, slope):
    portions = [(1 << 20) // math.isqrt(rank ** slope) + 1 for rank in range(2, amount + 1)]
    spare, given = total - bound - (amount - 1), [1] * (amount - 1)
    while spare > 0:
        candidates = [i for i in range(amount - 1) if given[i] < bound]
        mass, budget = sum([portions[i] for i in candidates]), spare
        for i in candidates:
            extra = min(bound - given[i], max(1, budget * portions[i] // mass), spare)
            given[i] = given[i] + extra
            spare = spare - extra
    return np.array([bound] + given)


def ragged(stream_key, number_of, total, bound, skew):
    if number_of == 2:
        one = jax.random.randint(stream_key, (), max(1, total - bound), min(bound, total - 1) + 1)
        return jnp.stack([one, total - one])
    tallies = jnp.asarray(length_profile(number_of, total, bound, skew), jnp.int32)
    pairs = (number_of - 1) // 2
    donor, taker = tallies[1:1 + 2 * pairs:2], tallies[2:2 + 2 * pairs:2]
    margin = jnp.minimum(donor - 1, bound - taker)
    passed = jax.random.randint(jax.random.fold_in(stream_key, 1), (pairs,), 0, 1 << 20) % (margin + 1)
    tallies = tallies.at[1:1 + 2 * pairs:2].set(donor - passed).at[2:2 + 2 * pairs:2].set(taker + passed)
    return tallies[jax.random.permutation(jax.random.fold_in(stream_key, 2), number_of)]


def gaussian(stream_key, dims, deviation, bound, split=(), dtype=jnp.bfloat16):
    entries = jax.random.normal(stream_key, dims, jnp.float32) * deviation
    if len(split) > 0:
        entries = block_levels(stream_key, dims, split, -0.22, 0.18) * entries
    return jnp.clip(entries, min=-bound, max=bound).astype(dtype)


def setup_inputs(seed: int = 0) -> dict:
    key_list = jax.random.split(jax.random.key(seed), 7)
    return {
        "attn_out": gaussian(key_list[0], (N_REPLICA, TOK, HEADS * HD), 1.0, 6.0, ((0, 32), (2, 32))),
        "proj": gaussian(key_list[1], (N_REPLICA, HEADS * HD, DW), 1.0, 6.0, ((0, 32), (1, 32))),
        "momentum": gaussian(key_list[2], (N_REPLICA, HEADS * HD, DW), 1.0, 6.0, ((0, 32), (1, 32))),
        "target": gaussian(key_list[3], (N_REPLICA, TOK, DW), 1.0, 6.0, ((0, 32),)),
        "segment_ids": jax.vmap(lambda own: jnp.searchsorted(jnp.cumsum(ragged(own, SEGS, TOK, SEG_MOST, 2)), jnp.arange(TOK), side="right"))(jax.random.split(key_list[4], N_REPLICA)).reshape((N_REPLICA, TOK)).astype(jnp.int32),
        "step": jax.random.randint(key_list[5], (1,), 0, 1000).astype(jnp.int32),
    }


BETA_MOM = 0.9
STEP_RATE = 0.1


def replica_step(inputs):
    heads_in, weight, moment_in, target_rows, seg_rows = inputs
    head_rows = HEADS_DEV * HD
    scaling = (HEADS * HD) ** -0.5
    blocks_in = heads_in.reshape(TOK, N_TENSOR, head_rows).transpose(1, 0, 2).astype(jnp.float32)
    blocks_w = weight.reshape(N_TENSOR, head_rows, DW).astype(jnp.float32)
    partial_terms = jnp.einsum("ntr,nrd->ntd", blocks_in, blocks_w, precision=lax.Precision.HIGHEST) * scaling
    summed = jnp.sum(partial_terms, axis=0)
    same_doc = (seg_rows[:, None] == seg_rows[None, :]).astype(jnp.float32)
    doc_sizes = jnp.sum(same_doc, axis=1)
    weights = TOK / (SEGS * doc_sizes)
    out_grad = ((summed - target_rows.astype(jnp.float32)) * weights[:, None]).astype(jnp.bfloat16)
    gradient = jnp.dot(heads_in.T, out_grad, preferred_element_type=jnp.float32) * scaling
    attn_grad = (jnp.dot(out_grad, weight.T, preferred_element_type=jnp.float32) * scaling).astype(jnp.bfloat16)
    moment = (BETA_MOM * moment_in.astype(jnp.float32) + gradient).astype(jnp.bfloat16)
    updated = (weight.astype(jnp.float32) - STEP_RATE * moment.astype(jnp.float32)).astype(jnp.bfloat16)
    return summed.astype(jnp.bfloat16), attn_grad, updated, moment


def reference(attn_out, proj, momentum, target, segment_ids, step):
    projected, attn_grad, updated, moment = lax.map(replica_step, (attn_out, proj, momentum, target, segment_ids))
    levels = N_REPLICA.bit_length() - 1
    chosen = (step[0] % levels).astype(jnp.int32)
    hop = jnp.left_shift(jnp.int32(1), chosen)
    partner_proj = jnp.roll(updated, hop, axis=0)
    partner_moment = jnp.roll(moment, hop, axis=0)
    new_proj = ((updated.astype(jnp.float32) + partner_proj.astype(jnp.float32)) * 0.5).astype(jnp.bfloat16)
    new_moment = ((moment.astype(jnp.float32) + partner_moment.astype(jnp.float32)) * 0.5).astype(jnp.bfloat16)
    return projected, attn_grad, new_proj, new_moment
```

```python
from functools import partial

import jax
import jax.numpy as jnp
from jax import lax
from jax.experimental import pallas as pl
from jax.experimental.pallas import tpu as pltpu
from jax.sharding import PartitionSpec as P

SEGS = 96
BETA_MOM = 0.9
STEP_RATE = 0.1
NX = 4
COLS = 2


def vmem(count):
    return [pl.BlockSpec(memory_space=pltpu.VMEM)] * count


def shift_z(x, by):
    size = lax.axis_size("tensor")
    return lax.ppermute(x, "tensor", [(i, (i + by * NX) % size) for i in range(size)])


def swap_x(x, k):
    size = lax.axis_size("tensor")
    return lax.ppermute(x, "tensor", [(i, i ^ k) for i in range(size)])


def pass_replica(x, by):
    size = lax.axis_size("replica")
    return lax.ppermute(x, "replica", [(i, (i + by) % size) for i in range(size)])


def place_of(j, k, z, x, nz):
    return lax.rem(z + j, nz) * NX + (x ^ k)


def order_kernel(nz, place_ref, rows_ref, out_ref):
    for j in range(nz):
        for k in range(NX):
            out_ref[j * NX + k] = rows_ref[place_of(j, k, place_ref[0], place_ref[1], nz)]


def moment_kernel(scaling, nz, *refs):
    heads_ref, blocks, mom_ref, out_ref, held = refs[0], refs[1 : 1 + nz], refs[-3], refs[-2], refs[-1]
    rows = blocks[0].shape[0]
    for j in range(nz):
        held[j * rows : (j + 1) * rows, :] = blocks[j][...]
    total = lax.dot_general(
        heads_ref[...], held[...], (((0,), (0,)), ((), ())), preferred_element_type=jnp.float32
    )
    out_ref[...] = (BETA_MOM * mom_ref[...].astype(jnp.float32) + total * scaling).astype(jnp.bfloat16)


def moment_of(heads, blocks, mom, scaling):
    nz, (rows, cols) = len(blocks), blocks[0].shape
    tile = min(512, cols)
    deep = heads.shape[1]
    column = lambda n: pl.BlockSpec((n, tile), lambda i: (0, i))
    return pl.pallas_call(
        partial(moment_kernel, scaling, nz),
        grid=(cols // tile,),
        out_shape=jax.ShapeDtypeStruct((deep, cols), jnp.bfloat16),
        in_specs=[pl.BlockSpec(heads.shape, lambda i: (0, 0))] + [column(rows)] * nz + [column(deep)],
        out_specs=column(deep),
        scratch_shapes=[pltpu.VMEM((nz * rows, tile), jnp.bfloat16)],
        cost_estimate=pl.CostEstimate(
            flops=2 * heads.size * cols, bytes_accessed=2 * (nz * rows * cols + 2 * deep * cols), transcendentals=0
        ),
        name="moment",
    )(heads, *blocks, mom)


def back_kernel(scaling, nz, parts, place_ref, *refs):
    w_ref, out_ref = refs[-2], refs[-1]
    cols = w_ref.shape[1] // parts
    for j in range(nz):
        total = None
        for c in range(parts):
            term = lax.dot_general(
                refs[c * nz + j][...],
                w_ref[:, c * cols : (c + 1) * cols],
                (((1,), (1,)), ((), ())),
                preferred_element_type=jnp.float32,
            )
            total = term if total is None else total + term
        rows = out_ref.shape[1]
        for k in range(NX):
            out_ref[place_of(j, k, place_ref[0], place_ref[1], nz)] = (
                total[k * rows : (k + 1) * rows] * scaling
            ).astype(jnp.bfloat16)


def on_device(hop, heads_in, weight, moment_in, target_rows, seg_rows):
    tokens, deep = heads_in.shape
    width = weight.shape[1]
    size = lax.axis_size("tensor")
    nz, rows = size // NX, tokens // size
    scaling = (deep * size) ** (-0.5)
    own = lax.axis_index("tensor")
    place = jnp.stack([own // NX, own % NX]).astype(jnp.int32)
    smem = pl.BlockSpec(memory_space=pltpu.SMEM)

    with jax.named_scope("early_partner"):
        partner_w = pass_replica(weight, hop)
    with jax.named_scope("order"):
        heads = pl.pallas_call(
            partial(order_kernel, nz),
            out_shape=jax.ShapeDtypeStruct((size, rows, deep), jnp.bfloat16),
            in_specs=[smem] + vmem(1),
            out_specs=vmem(1)[0],
            name="order",
        )(place, heads_in.reshape(size, rows, deep)).reshape(tokens, deep)
    first_row = own * rows
    own_seg = lax.dynamic_slice_in_dim(seg_rows, first_row, rows, 0)
    doc_sizes = jnp.sum((own_seg[:, None] == seg_rows[None, :]).astype(jnp.float32), axis=1)
    own_weights = (tokens / (SEGS * doc_sizes))[:, None]
    own_targets = lax.dynamic_slice_in_dim(target_rows, first_row, rows, 0).astype(jnp.float32)

    cols = width // COLS
    chunk = rows * NX
    sums, grads, blocks = [], [], []
    for c in range(COLS):
        part = slice(c * cols, (c + 1) * cols)
        up_steps, down_steps = (nz // 2, nz // 2 - 1) if c % 2 == 0 else (nz // 2 - 1, nz // 2)

        def share(j):
            j = j % nz
            return scaling * jnp.dot(
                heads[j * chunk : (j + 1) * chunk], weight[:, part], preferred_element_type=jnp.float32
            )

        with jax.named_scope("sum_z"):
            total = share(0)
            flows = [[1, up_steps, None], [-1, down_steps, None]]
            for s in range(nz // 2):
                for flow in flows:
                    way, steps, cur = flow
                    if s < steps:
                        term = share(way * (steps - s))
                        if cur is not None:
                            term = term + cur.astype(jnp.float32)
                        flow[2] = shift_z(term.astype(jnp.bfloat16), way)
            total = total + flows[0][2].astype(jnp.float32) + flows[1][2].astype(jnp.float32)
        with jax.named_scope("sum_x"):
            mine = total[:rows]
            for k in range(1, NX):
                sent = swap_x(total[k * rows : (k + 1) * rows].astype(jnp.bfloat16), k)
                mine = mine + sent.astype(jnp.float32)
        sums.append(mine.astype(jnp.bfloat16))
        grad = ((mine - own_targets[:, part]) * own_weights).astype(jnp.bfloat16)
        with jax.named_scope("gather_x"):
            block = jnp.concatenate([grad] + [swap_x(grad, k) for k in range(1, NX)], axis=0)
        with jax.named_scope("gather_z"):
            held = [block] + [None] * (nz - 1)
            flows = [[1, up_steps, block], [-1, down_steps, block]]
            for s in range(nz // 2):
                for flow in flows:
                    way, steps, cur = flow
                    if s < steps:
                        flow[2] = shift_z(cur, way)
                        held[(-way * (s + 1)) % nz] = flow[2]
        blocks.append(held)

    new_w, new_m = [], []
    for c in range(COLS):
        part = slice(c * cols, (c + 1) * cols)
        moment = moment_of(heads, blocks[c], moment_in[:, part], scaling)
        with jax.named_scope("partner"):
            partner_m = pass_replica(moment, hop).astype(jnp.float32)
        moment = moment.astype(jnp.float32)
        updated = (weight[:, part].astype(jnp.float32) - STEP_RATE * moment).astype(jnp.bfloat16)
        partner_u = (partner_w[:, part].astype(jnp.float32) - STEP_RATE * partner_m).astype(jnp.bfloat16)
        new_w.append(((updated.astype(jnp.float32) + partner_u.astype(jnp.float32)) * 0.5).astype(jnp.bfloat16))
        new_m.append(((moment + partner_m) * 0.5).astype(jnp.bfloat16))
    with jax.named_scope("back"):
        attn_grad = pl.pallas_call(
            partial(back_kernel, scaling, nz, COLS),
            out_shape=jax.ShapeDtypeStruct((size, rows, deep), jnp.bfloat16),
            in_specs=[smem] + vmem(nz * COLS + 1),
            out_specs=vmem(1)[0],
            cost_estimate=pl.CostEstimate(
                flops=2 * tokens * width * deep, bytes_accessed=2 * tokens * width, transcendentals=0
            ),
            name="back",
        )(place, *[b for held in blocks for b in held], weight).reshape(tokens, deep)
    join = lambda pieces: jnp.concatenate(pieces, axis=1)
    return join(sums), attn_grad, join(new_w), join(new_m)


def program(attn_out, proj, momentum, target, segment_ids, step):
    levels = lax.axis_size("replica").bit_length() - 1
    branches = [partial(on_device, 1 << bit) for bit in range(levels)]
    outs = lax.switch(
        step[0] % levels, branches, attn_out[0], proj[0], momentum[0], target[0], segment_ids[0]
    )
    return tuple(out[None] for out in outs)


def solution(mesh):
    return jax.shard_map(
        program,
        mesh=mesh,
        in_specs=(
            P("replica", None, "tensor"),
            P("replica", "tensor", None),
            P("replica", "tensor", None),
            P("replica", None, None),
            P("replica", None),
            P(),
        ),
        out_specs=(
            P("replica", "tensor", None),
            P("replica", None, "tensor"),
            P("replica", "tensor", None),
            P("replica", "tensor", None),
        ),
        check_vma=False,
    )
```

```python
from functools import partial

import jax
import jax.numpy as jnp
from jax import lax
from jax.experimental import pallas as pl
from jax.experimental.pallas import tpu as pltpu
from jax.sharding import PartitionSpec as P

SEGS = 96
BETA_MOM = 0.9
STEP_RATE = 0.1
NX = 4
PARTS = 2
SCALARS = pl.BlockSpec(memory_space=pltpu.SMEM)


def vmem(count):
    return [pl.BlockSpec(memory_space=pltpu.VMEM)] * count


def shift_z(x, by):
    size = lax.axis_size("tensor")
    return lax.ppermute(x, "tensor", [(i, (i + by * NX) % size) for i in range(size)])


def swap_x(x, k):
    size = lax.axis_size("tensor")
    return lax.ppermute(x, "tensor", [(i, i ^ k) for i in range(size)])


def pass_replica(x, by):
    size = lax.axis_size("replica")
    return lax.ppermute(x, "replica", [(i, (i + by) % size) for i in range(size)])


def place_of(j, k, z, x, nz):
    return lax.rem(z + j, nz) * NX + (x ^ k)


def order_kernel(nz, place_ref, rows_ref, out_ref):
    for j in range(nz):
        for k in range(NX):
            out_ref[j * NX + k] = rows_ref[place_of(j, k, place_ref[0], place_ref[1], nz)]


def moment_kernel(scaling, nz, *refs):
    heads_ref, blocks, mom_ref, out_ref, held = refs[0], refs[1 : 1 + nz], refs[-3], refs[-2], refs[-1]
    rows = blocks[0].shape[0]
    for j in range(nz):
        held[j * rows : (j + 1) * rows, :] = blocks[j][...]
    total = lax.dot_general(
        heads_ref[...], held[...], (((0,), (0,)), ((), ())), preferred_element_type=jnp.float32
    )
    out_ref[...] = (BETA_MOM * mom_ref[...].astype(jnp.float32) + total * scaling).astype(jnp.bfloat16)


def moment_of(heads, blocks, mom, scaling, part):
    nz, (rows, width) = len(blocks), blocks[0].shape
    deep, cols = heads.shape[1], width // PARTS
    tile = min(512, cols)
    first = part * cols // tile
    column = lambda n: pl.BlockSpec((n, tile), lambda i: (0, first + i))
    return pl.pallas_call(
        partial(moment_kernel, scaling, nz),
        grid=(cols // tile,),
        out_shape=jax.ShapeDtypeStruct((deep, cols), jnp.bfloat16),
        in_specs=[pl.BlockSpec(heads.shape, lambda i: (0, 0))] + [column(rows)] * nz + [column(deep)],
        out_specs=pl.BlockSpec((deep, tile), lambda i: (0, i)),
        scratch_shapes=[pltpu.VMEM((nz * rows, tile), jnp.bfloat16)],
        cost_estimate=pl.CostEstimate(
            flops=2 * heads.size * cols, bytes_accessed=2 * (nz * rows * cols + 2 * deep * cols), transcendentals=0
        ),
        name="moment",
    )(heads, *blocks, mom)


def back_kernel(scaling, nz, place_ref, *refs):
    w_ref, out_ref = refs[-2], refs[-1]
    rows = out_ref.shape[1]
    for j in range(nz):
        total = lax.dot_general(
            refs[j][...], w_ref[...], (((1,), (1,)), ((), ())), preferred_element_type=jnp.float32
        )
        for k in range(NX):
            out_ref[place_of(j, k, place_ref[0], place_ref[1], nz)] = (
                total[k * rows : (k + 1) * rows] * scaling
            ).astype(jnp.bfloat16)


def sum_stage(heads_in, weight, target_rows, seg_rows):
    tokens, deep = heads_in.shape
    size = lax.axis_size("tensor")
    nz, rows = size // NX, tokens // size
    chunk = rows * NX
    scaling = (deep * size) ** (-0.5)
    own = lax.axis_index("tensor")
    place = jnp.stack([own // NX, own % NX]).astype(jnp.int32)
    with jax.named_scope("order"):
        heads = pl.pallas_call(
            partial(order_kernel, nz),
            out_shape=jax.ShapeDtypeStruct((size, rows, deep), jnp.bfloat16),
            in_specs=[SCALARS] + vmem(1),
            out_specs=vmem(1)[0],
            name="order",
        )(place, heads_in.reshape(size, rows, deep)).reshape(tokens, deep)
    first_row = own * rows
    own_seg = lax.dynamic_slice_in_dim(seg_rows, first_row, rows, 0)
    doc_sizes = jnp.sum((own_seg[:, None] == seg_rows[None, :]).astype(jnp.float32), axis=1)
    own_weights = (tokens / (SEGS * doc_sizes))[:, None]
    own_targets = lax.dynamic_slice_in_dim(target_rows, first_row, rows, 0).astype(jnp.float32)

    def share(j):
        j = j % nz
        return scaling * jnp.dot(
            heads[j * chunk : (j + 1) * chunk], weight, preferred_element_type=jnp.float32
        )

    with jax.named_scope("sum_z"):
        total = share(0)
        flows = [[1, nz // 2, None], [-1, nz // 2 - 1, None]]
        for s in range(nz // 2):
            for flow in flows:
                way, steps, cur = flow
                if s < steps:
                    term = share(way * (steps - s))
                    if cur is not None:
                        term = term + cur.astype(jnp.float32)
                    flow[2] = shift_z(term.astype(jnp.bfloat16), way)
        total = total + flows[0][2].astype(jnp.float32) + flows[1][2].astype(jnp.float32)
    with jax.named_scope("sum_x"):
        mine = total[:rows]
        for k in range(1, NX):
            sent = swap_x(total[k * rows : (k + 1) * rows].astype(jnp.bfloat16), k)
            mine = mine + sent.astype(jnp.float32)
    grad = ((mine - own_targets) * own_weights).astype(jnp.bfloat16)
    return mine.astype(jnp.bfloat16), grad, heads, place


def update_stage(hop, grad, heads, place, weight, moment_in):
    tokens, deep = heads.shape
    rows, width = grad.shape
    size = lax.axis_size("tensor")
    nz = size // NX
    scaling = (deep * size) ** (-0.5)
    with jax.named_scope("early_partner"):
        partner_w = pass_replica(weight, hop)
    with jax.named_scope("gather_x"):
        block = jnp.concatenate([grad] + [swap_x(grad, k) for k in range(1, NX)], axis=0)
    with jax.named_scope("gather_z"):
        held = [block] + [None] * (nz - 1)
        flows = [[1, nz // 2, block], [-1, nz // 2 - 1, block]]
        for s in range(nz // 2):
            for flow in flows:
                way, steps, cur = flow
                if s < steps:
                    if s == nz // 2 - 2 and way == 1:
                        cur, partner_w = lax.optimization_barrier((cur, partner_w))
                    flow[2] = shift_z(cur, way)
                    held[(-way * (s + 1)) % nz] = flow[2]
    new_w, new_m = [], []
    cols = width // PARTS
    for c in range(PARTS):
        part = slice(c * cols, (c + 1) * cols)
        moment = moment_of(heads, held, moment_in, scaling, c)
        with jax.named_scope("partner"):
            partner_m = pass_replica(moment, hop).astype(jnp.float32)
        moment = moment.astype(jnp.float32)
        updated = (weight[:, part].astype(jnp.float32) - STEP_RATE * moment).astype(jnp.bfloat16)
        partner_u = (partner_w[:, part].astype(jnp.float32) - STEP_RATE * partner_m).astype(jnp.bfloat16)
        new_w.append(((updated.astype(jnp.float32) + partner_u.astype(jnp.float32)) * 0.5).astype(jnp.bfloat16))
        new_m.append(((moment + partner_m) * 0.5).astype(jnp.bfloat16))
    with jax.named_scope("back"):
        attn_grad = pl.pallas_call(
            partial(back_kernel, scaling, nz),
            out_shape=jax.ShapeDtypeStruct((size, rows, deep), jnp.bfloat16),
            in_specs=[SCALARS] + vmem(nz + 1),
            out_specs=vmem(1)[0],
            cost_estimate=pl.CostEstimate(
                flops=2 * tokens * width * deep, bytes_accessed=2 * tokens * width, transcendentals=0
            ),
            name="back",
        )(place, *held, weight).reshape(tokens, deep)
    join = lambda pieces: jnp.concatenate(pieces, axis=1)
    return attn_grad, join(new_w), join(new_m)


def program(attn_out, proj, momentum, target, segment_ids, step):
    levels = lax.axis_size("replica").bit_length() - 1
    projected, grad, heads, place = sum_stage(attn_out[0], proj[0], target[0], segment_ids[0])
    branches = [partial(update_stage, 1 << bit) for bit in range(levels)]
    outs = lax.switch(step[0] % levels, branches, grad, heads, place, proj[0], momentum[0])
    return tuple(out[None] for out in (projected, *outs))


def solution(mesh):
    return jax.shard_map(
        program,
        mesh=mesh,
        in_specs=(
            P("replica", None, "tensor"),
            P("replica", "tensor", None),
            P("replica", "tensor", None),
            P("replica", None, None),
            P("replica", None),
            P(),
        ),
        out_specs=(
            P("replica", "tensor", None),
            P("replica", None, "tensor"),
            P("replica", "tensor", None),
            P("replica", "tensor", None),
        ),
        check_vma=False,
    )
```

```python
from functools import partial

import jax
import jax.numpy as jnp
from jax import lax
from jax.experimental import pallas as pl
from jax.experimental.pallas import tpu as pltpu
from jax.sharding import PartitionSpec as P

SEGS = 96
BETA_MOM = 0.9
STEP_RATE = 0.1
NX = 4
SCALARS = pl.BlockSpec(memory_space=pltpu.SMEM)


def vmem(count):
    return [pl.BlockSpec(memory_space=pltpu.VMEM)] * count


def swap_z(x, odd):
    size = lax.axis_size("tensor")
    step = lambda i: -NX if (i // NX + odd) % 2 else NX
    return lax.ppermute(x, "tensor", [(i, (i + step(i)) % size) for i in range(size)])


def swap_x(x, k):
    size = lax.axis_size("tensor")
    return lax.ppermute(x, "tensor", [(i, i ^ k) for i in range(size)])


def pass_replica(x, by):
    size = lax.axis_size("replica")
    return lax.ppermute(x, "replica", [(i, (i + by) % size) for i in range(size)])


def place_of(j, k, z, x, nz):
    return lax.rem(z + (1 - 2 * lax.rem(z, 2)) * j + nz, nz) * NX + (x ^ k)


def order_kernel(nz, place_ref, rows_ref, out_ref):
    for j in range(nz):
        for k in range(NX):
            out_ref[j * NX + k] = rows_ref[place_of(j, k, place_ref[0], place_ref[1], nz)]


def moment_kernel(scaling, nz, *refs):
    heads_ref, blocks, mom_ref, out_ref, held = refs[0], refs[1 : 1 + nz], refs[-3], refs[-2], refs[-1]
    rows = blocks[0].shape[0]
    for j in range(nz):
        held[j * rows : (j + 1) * rows, :] = blocks[j][...]
    total = lax.dot_general(
        heads_ref[...], held[...], (((0,), (0,)), ((), ())), preferred_element_type=jnp.float32
    )
    out_ref[...] = (BETA_MOM * mom_ref[...].astype(jnp.float32) + total * scaling).astype(jnp.bfloat16)


def moment_of(heads, blocks, mom, scaling, part):
    nz, (rows, width) = len(blocks), blocks[0].shape
    deep, cols = heads.shape[1], width // 2
    tile = min(512, cols)
    first = part * cols // tile
    column = lambda n: pl.BlockSpec((n, tile), lambda i: (0, first + i))
    own = lambda n: pl.BlockSpec((n, tile), lambda i: (0, i))
    return pl.pallas_call(
        partial(moment_kernel, scaling, nz),
        grid=(cols // tile,),
        out_shape=jax.ShapeDtypeStruct((deep, cols), jnp.bfloat16),
        in_specs=[pl.BlockSpec(heads.shape, lambda i: (0, 0))]
        + [own(rows) if j == nz // 2 else column(rows) for j in range(nz)]
        + [column(deep)],
        out_specs=own(deep),
        scratch_shapes=[pltpu.VMEM((nz * rows, tile), jnp.bfloat16)],
        cost_estimate=pl.CostEstimate(
            flops=2 * heads.size * cols, bytes_accessed=2 * (nz * rows * cols + 2 * deep * cols), transcendentals=0
        ),
        name="moment",
    )(heads, *[b[part] if isinstance(b, tuple) else b for b in blocks], mom)


def back_kernel(scaling, nz, place_ref, *refs):
    w_ref, out_ref = refs[-2], refs[-1]
    rows, half = out_ref.shape[1], w_ref.shape[1] // 2
    times = lambda a, w: lax.dot_general(
        a, w, (((1,), (1,)), ((), ())), preferred_element_type=jnp.float32
    )
    for j in range(nz):
        if j == nz // 2:
            total = times(refs[j][...], w_ref[:, :half]) + times(refs[nz][...], w_ref[:, half:])
        else:
            total = times(refs[j][...], w_ref[...])
        for k in range(NX):
            out_ref[place_of(j, k, place_ref[0], place_ref[1], nz)] = (
                total[k * rows : (k + 1) * rows] * scaling
            ).astype(jnp.bfloat16)


def sum_stage(heads_in, weight, target_rows, seg_rows):
    tokens, deep = heads_in.shape
    size = lax.axis_size("tensor")
    nz, rows = size // NX, tokens // size
    chunk = rows * NX
    scaling = (deep * size) ** (-0.5)
    own = lax.axis_index("tensor")
    place = jnp.stack([own // NX, own % NX]).astype(jnp.int32)
    with jax.named_scope("order"):
        heads = pl.pallas_call(
            partial(order_kernel, nz),
            out_shape=jax.ShapeDtypeStruct((size, rows, deep), jnp.bfloat16),
            in_specs=[SCALARS] + vmem(1),
            out_specs=vmem(1)[0],
            name="order",
        )(place, heads_in.reshape(size, rows, deep)).reshape(tokens, deep)
    first_row = own * rows
    own_seg = lax.dynamic_slice_in_dim(seg_rows, first_row, rows, 0)
    doc_sizes = jnp.sum((own_seg[:, None] == seg_rows[None, :]).astype(jnp.float32), axis=1)
    own_weights = (tokens / (SEGS * doc_sizes))[:, None]
    own_targets = lax.dynamic_slice_in_dim(target_rows, first_row, rows, 0).astype(jnp.float32)

    def share(j):
        j = j % nz
        return scaling * jnp.dot(
            heads[j * chunk : (j + 1) * chunk], weight, preferred_element_type=jnp.float32
        )

    with jax.named_scope("sum_z"):
        half = weight.shape[1] // 2
        term = share(nz // 2).astype(jnp.bfloat16)
        even, odd = swap_z(term[:, :half], 0), swap_z(term[:, half:], 1)
        even = jnp.pad(even.astype(jnp.float32), ((0, 0), (0, half)))
        odd = jnp.pad(odd.astype(jnp.float32), ((0, 0), (half, 0)))
        for m in range(nz // 2 - 1, 0, -1):
            to_even = (share(m) + odd).astype(jnp.bfloat16)
            to_odd = (share(-m) + even).astype(jnp.bfloat16)
            even, odd = swap_z(to_even, 0).astype(jnp.float32), swap_z(to_odd, 1).astype(jnp.float32)
        total = share(0) + even + odd
    with jax.named_scope("sum_x"):
        mine = total[:rows]
        for k in range(1, NX):
            sent = swap_x(total[k * rows : (k + 1) * rows].astype(jnp.bfloat16), k)
            mine = mine + sent.astype(jnp.float32)
    grad = ((mine - own_targets) * own_weights).astype(jnp.bfloat16)
    return mine.astype(jnp.bfloat16), grad, heads, place


def update_stage(hop, grad, heads, place, weight, moment_in):
    tokens, deep = heads.shape
    rows, width = grad.shape
    size = lax.axis_size("tensor")
    nz = size // NX
    scaling = (deep * size) ** (-0.5)
    with jax.named_scope("early_partner"):
        partner_w = pass_replica(weight, hop)
    with jax.named_scope("gather_x"):
        block = jnp.concatenate([grad] + [swap_x(grad, k) for k in range(1, NX)], axis=0)
    with jax.named_scope("gather_z"):
        held = [block] + [None] * (nz - 1)
        even = odd = block
        half = width // 2
        for m in range(1, nz // 2):
            if m == nz // 2 - 1:
                even, odd, partner_w = lax.optimization_barrier((even, odd, partner_w))
            even, odd = swap_z(odd, 0), swap_z(even, 1)
            held[m], held[-m] = even, odd
        held[nz // 2] = (swap_z(even[:, :half], 1), swap_z(odd[:, half:], 0))
    new_w, new_m = [], []
    cols = width // 2
    for c in range(2):
        part = slice(c * cols, (c + 1) * cols)
        moment = moment_of(heads, held, moment_in, scaling, c)
        with jax.named_scope("partner"):
            partner_m = pass_replica(moment, hop).astype(jnp.float32)
        moment = moment.astype(jnp.float32)
        updated = (weight[:, part].astype(jnp.float32) - STEP_RATE * moment).astype(jnp.bfloat16)
        partner_u = (partner_w[:, part].astype(jnp.float32) - STEP_RATE * partner_m).astype(jnp.bfloat16)
        new_w.append(((updated.astype(jnp.float32) + partner_u.astype(jnp.float32)) * 0.5).astype(jnp.bfloat16))
        new_m.append(((moment + partner_m) * 0.5).astype(jnp.bfloat16))
    with jax.named_scope("back"):
        attn_grad = pl.pallas_call(
            partial(back_kernel, scaling, nz),
            out_shape=jax.ShapeDtypeStruct((size, rows, deep), jnp.bfloat16),
            in_specs=[SCALARS] + vmem(nz + 2),
            out_specs=vmem(1)[0],
            cost_estimate=pl.CostEstimate(
                flops=2 * tokens * width * deep, bytes_accessed=2 * tokens * width, transcendentals=0
            ),
            name="back",
        )(place, *[h[0] if isinstance(h, tuple) else h for h in held], held[nz // 2][1], weight).reshape(tokens, deep)
    join = lambda pieces: jnp.concatenate(pieces, axis=1)
    return attn_grad, join(new_w), join(new_m)


def program(attn_out, proj, momentum, target, segment_ids, step):
    levels = lax.axis_size("replica").bit_length() - 1
    projected, grad, heads, place = sum_stage(attn_out[0], proj[0], target[0], segment_ids[0])
    branches = [partial(update_stage, 1 << bit) for bit in range(levels)]
    outs = lax.switch(step[0] % levels, branches, grad, heads, place, proj[0], momentum[0])
    return tuple(out[None] for out in (projected, *outs))


def solution(mesh):
    return jax.shard_map(
        program,
        mesh=mesh,
        in_specs=(
            P("replica", None, "tensor"),
            P("replica", "tensor", None),
            P("replica", "tensor", None),
            P("replica", None, None),
            P("replica", None),
            P(),
        ),
        out_specs=(
            P("replica", "tensor", None),
            P("replica", None, "tensor"),
            P("replica", "tensor", None),
            P("replica", "tensor", None),
        ),
        check_vma=False,
    )
```

```python
from functools import partial

import jax
import jax.numpy as jnp
from jax import lax
from jax.experimental import pallas as pl
from jax.experimental.pallas import tpu as pltpu
from jax.sharding import PartitionSpec as P

SEGS = 96
BETA_MOM = 0.9
STEP_RATE = 0.1
NX = 4
SCALARS = pl.BlockSpec(memory_space=pltpu.SMEM)


def vmem(count):
    return [pl.BlockSpec(memory_space=pltpu.VMEM)] * count


def swap_z(x, odd):
    size = lax.axis_size("tensor")
    step = lambda i: -NX if (i // NX + odd) % 2 else NX
    return lax.ppermute(x, "tensor", [(i, (i + step(i)) % size) for i in range(size)])


def exchange_x(x):
    size = lax.axis_size("tensor")
    runs = [list(range(i, i + NX)) for i in range(0, size, NX)]
    return lax.all_to_all(x, "tensor", 0, 0, axis_index_groups=runs, tiled=True)


def pass_replica(x, by):
    size = lax.axis_size("replica")
    return lax.ppermute(x, "replica", [(i, (i + by) % size) for i in range(size)])


def place_of(j, k, z, nz):
    return lax.rem(z + (1 - 2 * lax.rem(z, 2)) * j + nz, nz) * NX + k


def order_kernel(nz, place_ref, rows_ref, out_ref):
    for j in range(nz):
        for k in range(NX):
            out_ref[j * NX + k] = rows_ref[place_of(j, k, place_ref[0], nz)]


def moment_kernel(scaling, nz, *refs):
    heads_ref, blocks, mom_ref, out_ref, held = refs[0], refs[1 : 1 + nz], refs[-3], refs[-2], refs[-1]
    rows = blocks[0].shape[0]
    for j in range(nz):
        held[j * rows : (j + 1) * rows, :] = blocks[j][...]
    total = lax.dot_general(
        heads_ref[...], held[...], (((0,), (0,)), ((), ())), preferred_element_type=jnp.float32
    )
    out_ref[...] = (BETA_MOM * mom_ref[...].astype(jnp.float32) + total * scaling).astype(jnp.bfloat16)


def moment_of(heads, blocks, mom, scaling, part):
    nz, (rows, width) = len(blocks), blocks[0].shape
    deep, cols = heads.shape[1], width // 2
    tile = min(512, cols)
    first = part * cols // tile
    column = lambda n: pl.BlockSpec((n, tile), lambda i: (0, first + i))
    own = lambda n: pl.BlockSpec((n, tile), lambda i: (0, i))
    return pl.pallas_call(
        partial(moment_kernel, scaling, nz),
        grid=(cols // tile,),
        out_shape=jax.ShapeDtypeStruct((deep, cols), jnp.bfloat16),
        in_specs=[pl.BlockSpec(heads.shape, lambda i: (0, 0))]
        + [own(rows) if j == nz // 2 else column(rows) for j in range(nz)]
        + [column(deep)],
        out_specs=own(deep),
        scratch_shapes=[pltpu.VMEM((nz * rows, tile), jnp.bfloat16)],
        cost_estimate=pl.CostEstimate(
            flops=2 * heads.size * cols, bytes_accessed=2 * (nz * rows * cols + 2 * deep * cols), transcendentals=0
        ),
        name="moment",
    )(heads, *[b[part] if isinstance(b, tuple) else b for b in blocks], mom)


def back_kernel(scaling, nz, place_ref, *refs):
    w_ref, out_ref = refs[-2], refs[-1]
    rows, half = out_ref.shape[1], w_ref.shape[1] // 2
    times = lambda a, w: lax.dot_general(
        a, w, (((1,), (1,)), ((), ())), preferred_element_type=jnp.float32
    )
    for j in range(nz):
        if j == nz // 2:
            total = times(refs[j][...], w_ref[:, :half]) + times(refs[nz][...], w_ref[:, half:])
        else:
            total = times(refs[j][...], w_ref[...])
        for k in range(NX):
            out_ref[place_of(j, k, place_ref[0], nz)] = (
                total[k * rows : (k + 1) * rows] * scaling
            ).astype(jnp.bfloat16)


def sum_stage(heads_in, weight, target_rows, seg_rows):
    tokens, deep = heads_in.shape
    size = lax.axis_size("tensor")
    nz, rows = size // NX, tokens // size
    chunk = rows * NX
    scaling = (deep * size) ** (-0.5)
    own = lax.axis_index("tensor")
    place = (own // NX).astype(jnp.int32)[None]
    with jax.named_scope("order"):
        heads = pl.pallas_call(
            partial(order_kernel, nz),
            out_shape=jax.ShapeDtypeStruct((size, rows, deep), jnp.bfloat16),
            in_specs=[SCALARS] + vmem(1),
            out_specs=vmem(1)[0],
            name="order",
        )(place, heads_in.reshape(size, rows, deep)).reshape(tokens, deep)
    first_row = own * rows
    own_seg = lax.dynamic_slice_in_dim(seg_rows, first_row, rows, 0)
    doc_sizes = jnp.sum((own_seg[:, None] == seg_rows[None, :]).astype(jnp.float32), axis=1)
    own_weights = (tokens / (SEGS * doc_sizes))[:, None]
    own_targets = lax.dynamic_slice_in_dim(target_rows, first_row, rows, 0).astype(jnp.float32)

    def share(j):
        j = j % nz
        return scaling * jnp.dot(
            heads[j * chunk : (j + 1) * chunk], weight, preferred_element_type=jnp.float32
        )

    with jax.named_scope("sum_z"):
        half = weight.shape[1] // 2
        term = share(nz // 2).astype(jnp.bfloat16)
        even, odd = swap_z(term[:, :half], 0), swap_z(term[:, half:], 1)
        even = jnp.pad(even.astype(jnp.float32), ((0, 0), (0, half)))
        odd = jnp.pad(odd.astype(jnp.float32), ((0, 0), (half, 0)))
        for m in range(nz // 2 - 1, 0, -1):
            to_even = (share(m) + odd).astype(jnp.bfloat16)
            to_odd = (share(-m) + even).astype(jnp.bfloat16)
            even, odd = swap_z(to_even, 0).astype(jnp.float32), swap_z(to_odd, 1).astype(jnp.float32)
        total = share(0) + even + odd
    with jax.named_scope("sum_x"):
        parts = exchange_x(total.astype(jnp.bfloat16)).reshape(NX, rows, -1)
        mine = jnp.sum(parts.astype(jnp.float32), axis=0)
    grad = ((mine - own_targets) * own_weights).astype(jnp.bfloat16)
    return mine.astype(jnp.bfloat16), grad, heads, place


def update_stage(hop, grad, heads, place, weight, moment_in):
    tokens, deep = heads.shape
    rows, width = grad.shape
    size = lax.axis_size("tensor")
    nz = size // NX
    scaling = (deep * size) ** (-0.5)
    with jax.named_scope("early_partner"):
        half = width // 2
        partner_w = [pass_replica(weight[:, :half], hop), pass_replica(weight[:, half:], hop)]
    with jax.named_scope("gather_x"):
        block = exchange_x(jnp.tile(grad, (NX, 1)))
    with jax.named_scope("gather_z"):
        held = [block] + [None] * (nz - 1)
        even = odd = block
        for m in range(1, nz // 2):
            if m == nz // 2 - 1:
                even, odd, partner_w[0] = lax.optimization_barrier((even, odd, partner_w[0]))
            even, odd = swap_z(odd, 0), swap_z(even, 1)
            held[m], held[-m] = even, odd
        even, odd, partner_w[1] = lax.optimization_barrier((even, odd, partner_w[1]))
        held[nz // 2] = (swap_z(even[:, :half], 1), swap_z(odd[:, half:], 0))
    new_w, new_m = [], []
    for c in range(2):
        part = slice(c * half, (c + 1) * half)
        moment = moment_of(heads, held, moment_in, scaling, c)
        with jax.named_scope("partner"):
            partner_m = pass_replica(moment, hop).astype(jnp.float32)
        moment = moment.astype(jnp.float32)
        updated = (weight[:, part].astype(jnp.float32) - STEP_RATE * moment).astype(jnp.bfloat16)
        partner_u = (partner_w[c].astype(jnp.float32) - STEP_RATE * partner_m).astype(jnp.bfloat16)
        new_w.append(((updated.astype(jnp.float32) + partner_u.astype(jnp.float32)) * 0.5).astype(jnp.bfloat16))
        new_m.append(((moment + partner_m) * 0.5).astype(jnp.bfloat16))
    with jax.named_scope("back"):
        attn_grad = pl.pallas_call(
            partial(back_kernel, scaling, nz),
            out_shape=jax.ShapeDtypeStruct((size, rows, deep), jnp.bfloat16),
            in_specs=[SCALARS] + vmem(nz + 2),
            out_specs=vmem(1)[0],
            cost_estimate=pl.CostEstimate(
                flops=2 * tokens * width * deep, bytes_accessed=2 * tokens * width, transcendentals=0
            ),
            name="back",
        )(place, *[h[0] if isinstance(h, tuple) else h for h in held], held[nz // 2][1], weight).reshape(tokens, deep)
    join = lambda pieces: jnp.concatenate(pieces, axis=1)
    return attn_grad, join(new_w), join(new_m)


def program(attn_out, proj, momentum, target, segment_ids, step):
    levels = lax.axis_size("replica").bit_length() - 1
    projected, grad, heads, place = sum_stage(attn_out[0], proj[0], target[0], segment_ids[0])
    branches = [partial(update_stage, 1 << bit) for bit in range(levels)]
    outs = lax.switch(step[0] % levels, branches, grad, heads, place, proj[0], momentum[0])
    return tuple(out[None] for out in (projected, *outs))


def solution(mesh):
    return jax.shard_map(
        program,
        mesh=mesh,
        in_specs=(
            P("replica", None, "tensor"),
            P("replica", "tensor", None),
            P("replica", "tensor", None),
            P("replica", None, None),
            P("replica", None),
            P(),
        ),
        out_specs=(
            P("replica", "tensor", None),
            P("replica", None, "tensor"),
            P("replica", "tensor", None),
            P("replica", "tensor", None),
        ),
        check_vma=False,
    )
```

```python
from functools import partial

import jax
import jax.numpy as jnp
from jax import lax
from jax.experimental import pallas as pl
from jax.experimental.pallas import tpu as pltpu
from jax.sharding import PartitionSpec as P

SEGS = 96
BETA_MOM = 0.9
STEP_RATE = 0.1
NX = 4
SCALARS = pl.BlockSpec(memory_space=pltpu.SMEM)


def vmem(count):
    return [pl.BlockSpec(memory_space=pltpu.VMEM)] * count


def swap_z(x, odd):
    size = lax.axis_size("tensor")
    step = lambda i: -NX if (i // NX + odd) % 2 else NX
    return lax.ppermute(x, "tensor", [(i, (i + step(i)) % size) for i in range(size)])


def exchange_x(x):
    size = lax.axis_size("tensor")
    runs = [list(range(i, i + NX)) for i in range(0, size, NX)]
    return lax.all_to_all(x, "tensor", 0, 0, axis_index_groups=runs, tiled=True)


def pass_replica(x, by):
    size = lax.axis_size("replica")
    return lax.ppermute(x, "replica", [(i, (i + by) % size) for i in range(size)])


def place_of(j, k, z, nz):
    return lax.rem(z + (1 - 2 * lax.rem(z, 2)) * j + nz, nz) * NX + k


def order_kernel(nz, place_ref, rows_ref, out_ref):
    for j in range(nz):
        for k in range(NX):
            out_ref[j * NX + k] = rows_ref[place_of(j, k, place_ref[0], nz)]


def times_rows(heads_ref, blocks, first, held):
    rows = blocks[0].shape[0]
    for j, block in enumerate(blocks):
        held[j * rows : (j + 1) * rows, :] = block[...]
    count = len(blocks) * rows
    return lax.dot_general(
        heads_ref[first * rows : first * rows + count, :],
        held[:count, :],
        (((0,), (0,)), ((), ())),
        preferred_element_type=jnp.float32,
    )


def near_kernel(nz, heads_ref, *refs):
    blocks, out_ref, held, other = refs[:-3], refs[-3], refs[-2], refs[-1]
    low = nz // 2 - 1
    out_ref[...] = times_rows(heads_ref, blocks[:low], 0, held) + times_rows(
        heads_ref, blocks[low:], nz // 2 + 2, other
    )


def moment_kernel(scaling, nz, heads_ref, *refs):
    blocks, near_ref, mom_ref, out_ref, held = refs[:-4], refs[-4], refs[-3], refs[-2], refs[-1]
    total = near_ref[...] + times_rows(heads_ref, blocks, nz // 2 - 1, held)
    out_ref[...] = (BETA_MOM * mom_ref[...].astype(jnp.float32) + total * scaling).astype(jnp.bfloat16)


def near_of(heads, blocks):
    nz, (rows, width) = len(blocks), blocks[0].shape
    deep = heads.shape[1]
    tile = min(512, width)
    near = [blocks[j] for j in range(nz) if abs(j - nz // 2) > 1]
    column = lambda n: pl.BlockSpec((n, tile), lambda i: (0, i))
    return pl.pallas_call(
        partial(near_kernel, nz),
        grid=(width // tile,),
        out_shape=jax.ShapeDtypeStruct((deep, width), jnp.float32),
        in_specs=[pl.BlockSpec(heads.shape, lambda i: (0, 0))] + [column(rows)] * len(near),
        out_specs=column(deep),
        scratch_shapes=[
            pltpu.VMEM(((nz // 2 - 1) * rows, tile), jnp.bfloat16),
            pltpu.VMEM(((nz // 2 - 2) * rows, tile), jnp.bfloat16),
        ],
        cost_estimate=pl.CostEstimate(
            flops=2 * deep * len(near) * rows * width, bytes_accessed=2 * len(near) * rows * width, transcendentals=0
        ),
        name="near",
    )(heads, *near)


def moment_of(heads, blocks, near, mom, scaling, part):
    nz, (rows, width) = len(blocks), blocks[0].shape
    deep, cols = heads.shape[1], width // 2
    tile = min(512, cols)
    first = part * cols // tile
    column = lambda n: pl.BlockSpec((n, tile), lambda i: (0, first + i))
    own = lambda n: pl.BlockSpec((n, tile), lambda i: (0, i))
    far = [blocks[nz // 2 - 1], blocks[nz // 2][part], blocks[nz // 2 + 1]]
    return pl.pallas_call(
        partial(moment_kernel, scaling, nz),
        grid=(cols // tile,),
        out_shape=jax.ShapeDtypeStruct((deep, cols), jnp.bfloat16),
        in_specs=[pl.BlockSpec(heads.shape, lambda i: (0, 0)), column(rows), own(rows), column(rows)]
        + [column(deep)] * 2,
        out_specs=own(deep),
        scratch_shapes=[pltpu.VMEM((len(far) * rows, tile), jnp.bfloat16)],
        cost_estimate=pl.CostEstimate(
            flops=2 * deep * len(far) * rows * cols, bytes_accessed=8 * deep * cols, transcendentals=0
        ),
        name="moment",
    )(heads, *far, near, mom)


def back_kernel(scaling, nz, place_ref, *refs):
    w_ref, out_ref = refs[-2], refs[-1]
    rows, half = out_ref.shape[1], w_ref.shape[1] // 2
    times = lambda a, w: lax.dot_general(
        a, w, (((1,), (1,)), ((), ())), preferred_element_type=jnp.float32
    )
    for j in range(nz):
        if j == nz // 2:
            total = times(refs[j][...], w_ref[:, :half]) + times(refs[nz][...], w_ref[:, half:])
        else:
            total = times(refs[j][...], w_ref[...])
        for k in range(NX):
            out_ref[place_of(j, k, place_ref[0], nz)] = (
                total[k * rows : (k + 1) * rows] * scaling
            ).astype(jnp.bfloat16)


def sum_stage(heads_in, weight, target_rows, seg_rows):
    tokens, deep = heads_in.shape
    size = lax.axis_size("tensor")
    nz, rows = size // NX, tokens // size
    chunk = rows * NX
    scaling = (deep * size) ** (-0.5)
    own = lax.axis_index("tensor")
    place = (own // NX).astype(jnp.int32)[None]
    with jax.named_scope("order"):
        heads = pl.pallas_call(
            partial(order_kernel, nz),
            out_shape=jax.ShapeDtypeStruct((size, rows, deep), jnp.bfloat16),
            in_specs=[SCALARS] + vmem(1),
            out_specs=vmem(1)[0],
            name="order",
        )(place, heads_in.reshape(size, rows, deep)).reshape(tokens, deep)
    first_row = own * rows
    own_seg = lax.dynamic_slice_in_dim(seg_rows, first_row, rows, 0)
    doc_sizes = jnp.sum((own_seg[:, None] == seg_rows[None, :]).astype(jnp.float32), axis=1)
    own_weights = (tokens / (SEGS * doc_sizes))[:, None]
    own_targets = lax.dynamic_slice_in_dim(target_rows, first_row, rows, 0).astype(jnp.float32)

    def share(j):
        j = j % nz
        return scaling * jnp.dot(
            heads[j * chunk : (j + 1) * chunk], weight, preferred_element_type=jnp.float32
        )

    with jax.named_scope("sum_z"):
        half = weight.shape[1] // 2
        term = share(nz // 2).astype(jnp.bfloat16)
        even, odd = swap_z(term[:, :half], 0), swap_z(term[:, half:], 1)
        even = jnp.pad(even.astype(jnp.float32), ((0, 0), (0, half)))
        odd = jnp.pad(odd.astype(jnp.float32), ((0, 0), (half, 0)))
        for m in range(nz // 2 - 1, 0, -1):
            to_even = (share(m) + odd).astype(jnp.bfloat16)
            to_odd = (share(-m) + even).astype(jnp.bfloat16)
            even, odd = swap_z(to_even, 0).astype(jnp.float32), swap_z(to_odd, 1).astype(jnp.float32)
        total = share(0) + even + odd
    with jax.named_scope("sum_x"):
        parts = exchange_x(total.astype(jnp.bfloat16)).reshape(NX, rows, -1)
        mine = jnp.sum(parts.astype(jnp.float32), axis=0)
    grad = ((mine - own_targets) * own_weights).astype(jnp.bfloat16)
    return mine.astype(jnp.bfloat16), grad, heads, place


def update_stage(hop, grad, heads, place, weight, moment_in):
    tokens, deep = heads.shape
    rows, width = grad.shape
    size = lax.axis_size("tensor")
    nz = size // NX
    scaling = (deep * size) ** (-0.5)
    with jax.named_scope("early_partner"):
        half = width // 2
        partner_w = pass_replica(weight, hop)
    with jax.named_scope("gather_x"):
        block = exchange_x(jnp.tile(grad, (NX, 1)))
    with jax.named_scope("gather_z"):
        held = [block] + [None] * (nz - 1)
        even = odd = block
        for m in range(1, nz // 2):
            even, odd = swap_z(odd, 0), swap_z(even, 1)
            held[m], held[-m] = even, odd
        near = near_of(heads, held)
        even = lax.optimization_barrier((near, even))[1]
        odd = lax.optimization_barrier((near, odd))[1]
        held[nz // 2] = (swap_z(even[:, :half], 1), swap_z(odd[:, half:], 0))
    new_w, new_m = [], []
    for c in range(2):
        part = slice(c * half, (c + 1) * half)
        if c == 1:
            moment_in, partner_w = lax.optimization_barrier((moment_in, partner_w))
        moment = moment_of(heads, held, near, moment_in, scaling, c)
        with jax.named_scope("partner"):
            partner_m = pass_replica(moment, hop).astype(jnp.float32)
        moment = moment.astype(jnp.float32)
        updated = (weight[:, part].astype(jnp.float32) - STEP_RATE * moment).astype(jnp.bfloat16)
        partner_u = (partner_w[:, part].astype(jnp.float32) - STEP_RATE * partner_m).astype(jnp.bfloat16)
        new_w.append(((updated.astype(jnp.float32) + partner_u.astype(jnp.float32)) * 0.5).astype(jnp.bfloat16))
        new_m.append(((moment + partner_m) * 0.5).astype(jnp.bfloat16))
    with jax.named_scope("back"):
        attn_grad = pl.pallas_call(
            partial(back_kernel, scaling, nz),
            out_shape=jax.ShapeDtypeStruct((size, rows, deep), jnp.bfloat16),
            in_specs=[SCALARS] + vmem(nz + 2),
            out_specs=vmem(1)[0],
            cost_estimate=pl.CostEstimate(
                flops=2 * tokens * width * deep, bytes_accessed=2 * tokens * width, transcendentals=0
            ),
            name="back",
        )(place, *[h[0] if isinstance(h, tuple) else h for h in held], held[nz // 2][1], weight).reshape(tokens, deep)
    join = lambda pieces: jnp.concatenate(pieces, axis=1)
    return attn_grad, join(new_w), join(new_m)


def program(attn_out, proj, momentum, target, segment_ids, step):
    levels = lax.axis_size("replica").bit_length() - 1
    projected, grad, heads, place = sum_stage(attn_out[0], proj[0], target[0], segment_ids[0])
    branches = [partial(update_stage, 1 << bit) for bit in range(levels)]
    outs = lax.switch(step[0] % levels, branches, grad, heads, place, proj[0], momentum[0])
    return tuple(out[None] for out in (projected, *outs))


def solution(mesh):
    return jax.shard_map(
        program,
        mesh=mesh,
        in_specs=(
            P("replica", None, "tensor"),
            P("replica", "tensor", None),
            P("replica", "tensor", None),
            P("replica", None, None),
            P("replica", None),
            P(),
        ),
        out_specs=(
            P("replica", "tensor", None),
            P("replica", None, "tensor"),
            P("replica", "tensor", None),
            P("replica", "tensor", None),
        ),
        check_vma=False,
    )
```

```python
from functools import partial

import jax
import jax.numpy as jnp
from jax import lax
from jax.experimental import pallas as pl
from jax.experimental.pallas import tpu as pltpu
from jax.sharding import PartitionSpec as P

SEGS = 96
BETA_MOM = 0.9
STEP_RATE = 0.1
NX = 4
SMALL = pltpu.CompilerParams(vmem_limit_bytes=16 << 20)
SCALARS = pl.BlockSpec(memory_space=pltpu.SMEM)


def vmem(count):
    return [pl.BlockSpec(memory_space=pltpu.VMEM)] * count


def swap_z(x, odd):
    size = lax.axis_size("tensor")
    step = lambda i: -NX if (i // NX + odd) % 2 else NX
    return lax.ppermute(x, "tensor", [(i, (i + step(i)) % size) for i in range(size)])


def exchange_x(x):
    size = lax.axis_size("tensor")
    runs = [list(range(i, i + NX)) for i in range(0, size, NX)]
    return lax.all_to_all(x, "tensor", 0, 0, axis_index_groups=runs, tiled=True)


def pass_replica(x, by):
    size = lax.axis_size("replica")
    return lax.ppermute(x, "replica", [(i, (i + by) % size) for i in range(size)])


def place_of(j, k, z, nz):
    return lax.rem(z + (1 - 2 * lax.rem(z, 2)) * j + nz, nz) * NX + k


def order_kernel(nz, place_ref, rows_ref, out_ref):
    for j in range(nz):
        for k in range(NX):
            out_ref[j * NX + k] = rows_ref[place_of(j, k, place_ref[0], nz)]


def times_rows(heads_ref, blocks, first, held):
    rows = blocks[0].shape[0]
    for j, block in enumerate(blocks):
        held[j * rows : (j + 1) * rows, :] = block
    count = len(blocks) * rows
    return lax.dot_general(
        heads_ref[first * rows : first * rows + count, :],
        held[:count, :],
        (((0,), (0,)), ((), ())),
        preferred_element_type=jnp.float32,
    )


def near_kernel(nz, heads_ref, *refs):
    blocks, out_ref, held, other = refs[:-3], refs[-3], refs[-2], refs[-1]
    low, tile = nz // 2 - 1, held.shape[1]
    for c in range(0, out_ref.shape[1], tile):
        part = [block[:, c : c + tile] for block in blocks]
        out_ref[:, c : c + tile] = times_rows(heads_ref, part[:low], 0, held) + times_rows(
            heads_ref, part[low:], nz // 2 + 2, other
        )


def moment_kernel(scaling, nz, first, heads_ref, *refs):
    blocks, near_ref, mom_ref, out_ref, held = refs[:-4], refs[-4], refs[-3], refs[-2], refs[-1]
    tile = held.shape[1]
    for c in range(0, out_ref.shape[1], tile):
        own, full = slice(c, c + tile), slice(first + c, first + c + tile)
        part = [blocks[0][:, full], blocks[1][:, own], blocks[2][:, full]]
        total = near_ref[:, full] + times_rows(heads_ref, part, nz // 2 - 1, held)
        out_ref[:, own] = (BETA_MOM * mom_ref[:, full].astype(jnp.float32) + total * scaling).astype(
            jnp.bfloat16
        )


def near_of(heads, blocks):
    nz, (rows, width) = len(blocks), blocks[0].shape
    deep = heads.shape[1]
    tile = min(512, width)
    near = [blocks[j] for j in range(nz) if abs(j - nz // 2) > 1]
    return pl.pallas_call(
        partial(near_kernel, nz),
        out_shape=jax.ShapeDtypeStruct((deep, width), jnp.float32),
        in_specs=vmem(1 + len(near)),
        out_specs=vmem(1)[0],
        scratch_shapes=[
            pltpu.VMEM(((nz // 2 - 1) * rows, tile), jnp.bfloat16),
            pltpu.VMEM(((nz // 2 - 2) * rows, tile), jnp.bfloat16),
        ],
        cost_estimate=pl.CostEstimate(
            flops=2 * deep * len(near) * rows * width, bytes_accessed=2 * len(near) * rows * width, transcendentals=0
        ),
        name="near",
        compiler_params=SMALL,
    )(heads, *near)


def moment_of(heads, blocks, near, mom, scaling, part):
    nz, (rows, width) = len(blocks), blocks[0].shape
    deep, cols = heads.shape[1], width // 2
    tile = min(512, cols)
    far = [blocks[nz // 2 - 1], blocks[nz // 2][part], blocks[nz // 2 + 1]]
    return pl.pallas_call(
        partial(moment_kernel, scaling, nz, part * cols),
        out_shape=jax.ShapeDtypeStruct((deep, cols), jnp.bfloat16),
        in_specs=vmem(3 + len(far)),
        out_specs=vmem(1)[0],
        scratch_shapes=[pltpu.VMEM((len(far) * rows, tile), jnp.bfloat16)],
        cost_estimate=pl.CostEstimate(
            flops=2 * deep * len(far) * rows * cols, bytes_accessed=8 * deep * cols, transcendentals=0
        ),
        name="moment",
        compiler_params=SMALL,
    )(heads, *far, near, mom)


def mix_kernel(*refs):
    w_ref, partner_w_ref, moments, new_w_ref, new_m_ref = refs[0], refs[1], refs[2:-2], refs[-2], refs[-1]
    wide = lambda x: x.astype(jnp.float32)
    narrow = lambda x: x.astype(jnp.bfloat16)
    half = moments[0].shape[1]
    for c in range(2):
        part = slice(c * half, (c + 1) * half)
        moment, partner_m = wide(moments[c][...]), wide(moments[2 + c][...])
        updated = narrow(wide(w_ref[:, part]) - STEP_RATE * moment)
        partner_u = narrow(wide(partner_w_ref[:, part]) - STEP_RATE * partner_m)
        new_w_ref[:, part] = narrow((wide(updated) + wide(partner_u)) * 0.5)
        new_m_ref[:, part] = narrow((moment + partner_m) * 0.5)


def back_kernel(scaling, nz, place_ref, *refs):
    w_ref, out_ref = refs[-2], refs[-1]
    rows, half = out_ref.shape[1], w_ref.shape[1] // 2
    times = lambda a, w: lax.dot_general(
        a, w, (((1,), (1,)), ((), ())), preferred_element_type=jnp.float32
    )
    for j in range(nz):
        if j == nz // 2:
            total = times(refs[j][...], w_ref[:, :half]) + times(refs[nz][...], w_ref[:, half:])
        else:
            total = times(refs[j][...], w_ref[...])
        for k in range(NX):
            out_ref[place_of(j, k, place_ref[0], nz)] = (
                total[k * rows : (k + 1) * rows] * scaling
            ).astype(jnp.bfloat16)


def sum_stage(heads_in, weight, target_rows, seg_rows):
    tokens, deep = heads_in.shape
    size = lax.axis_size("tensor")
    nz, rows = size // NX, tokens // size
    chunk = rows * NX
    scaling = (deep * size) ** (-0.5)
    own = lax.axis_index("tensor")
    place = (own // NX).astype(jnp.int32)[None]
    with jax.named_scope("order"):
        heads = pl.pallas_call(
            partial(order_kernel, nz),
            out_shape=jax.ShapeDtypeStruct((size, rows, deep), jnp.bfloat16),
            in_specs=[SCALARS] + vmem(1),
            out_specs=vmem(1)[0],
            name="order",
            compiler_params=SMALL,
        )(place, heads_in.reshape(size, rows, deep)).reshape(tokens, deep)
    first_row = own * rows
    own_seg = lax.dynamic_slice_in_dim(seg_rows, first_row, rows, 0)
    doc_sizes = jnp.sum((own_seg[:, None] == seg_rows[None, :]).astype(jnp.float32), axis=1)
    own_weights = (tokens / (SEGS * doc_sizes))[:, None]
    own_targets = lax.dynamic_slice_in_dim(target_rows, first_row, rows, 0).astype(jnp.float32)

    def share(j):
        j = j % nz
        return scaling * jnp.dot(
            heads[j * chunk : (j + 1) * chunk], weight, preferred_element_type=jnp.float32
        )

    with jax.named_scope("sum_z"):
        half = weight.shape[1] // 2
        term = share(nz // 2).astype(jnp.bfloat16)
        even, odd = swap_z(term[:, :half], 0), swap_z(term[:, half:], 1)
        even = jnp.pad(even.astype(jnp.float32), ((0, 0), (0, half)))
        odd = jnp.pad(odd.astype(jnp.float32), ((0, 0), (half, 0)))
        for m in range(nz // 2 - 1, 0, -1):
            to_even = (share(m) + odd).astype(jnp.bfloat16)
            to_odd = (share(-m) + even).astype(jnp.bfloat16)
            even, odd = swap_z(to_even, 0).astype(jnp.float32), swap_z(to_odd, 1).astype(jnp.float32)
        total = share(0) + even + odd
    with jax.named_scope("sum_x"):
        parts = exchange_x(total.astype(jnp.bfloat16)).reshape(NX, rows, -1)
        mine = jnp.sum(parts.astype(jnp.float32), axis=0)
    grad = ((mine - own_targets) * own_weights).astype(jnp.bfloat16)
    return mine.astype(jnp.bfloat16), grad, heads, place


def update_stage(hop, grad, heads, place, weight, moment_in):
    tokens, deep = heads.shape
    rows, width = grad.shape
    size = lax.axis_size("tensor")
    nz = size // NX
    scaling = (deep * size) ** (-0.5)
    with jax.named_scope("early_partner"):
        half = width // 2
        partner_w = pass_replica(weight, hop)
    with jax.named_scope("gather_x"):
        block = exchange_x(jnp.tile(grad, (NX, 1)))
    with jax.named_scope("gather_z"):
        held = [block] + [None] * (nz - 1)
        even = odd = block
        for m in range(1, nz // 2):
            if m == 2:
                even, odd, partner_w = lax.optimization_barrier((even, odd, partner_w))
            even, odd = swap_z(odd, 0), swap_z(even, 1)
            held[m], held[-m] = even, odd
        near = near_of(heads, held)
        even = lax.optimization_barrier((near, even))[1]
        odd = lax.optimization_barrier((near, odd))[1]
        held[nz // 2] = (swap_z(even[:, :half], 1), swap_z(odd[:, half:], 0))
    moments, partner_m = [], []
    for c in range(2):
        moments.append(moment_of(heads, held, near, moment_in, scaling, c))
        with jax.named_scope("partner"):
            partner_m.append(pass_replica(moments[c], hop))
    with jax.named_scope("mix"):
        new_w, new_m = pl.pallas_call(
            mix_kernel,
            out_shape=[jax.ShapeDtypeStruct(weight.shape, jnp.bfloat16)] * 2,
            in_specs=vmem(6),
            out_specs=vmem(2),
            name="mix",
            compiler_params=SMALL,
        )(weight, partner_w, *moments, *partner_m)
    with jax.named_scope("back"):
        attn_grad = pl.pallas_call(
            partial(back_kernel, scaling, nz),
            out_shape=jax.ShapeDtypeStruct((size, rows, deep), jnp.bfloat16),
            in_specs=[SCALARS] + vmem(nz + 2),
            out_specs=vmem(1)[0],
            cost_estimate=pl.CostEstimate(
                flops=2 * tokens * width * deep, bytes_accessed=2 * tokens * width, transcendentals=0
            ),
            name="back",
            compiler_params=SMALL,
        )(place, *[h[0] if isinstance(h, tuple) else h for h in held], held[nz // 2][1], weight).reshape(tokens, deep)
    return attn_grad, new_w, new_m


def program(attn_out, proj, momentum, target, segment_ids, step):
    levels = lax.axis_size("replica").bit_length() - 1
    projected, grad, heads, place = sum_stage(attn_out[0], proj[0], target[0], segment_ids[0])
    branches = [partial(update_stage, 1 << bit) for bit in range(levels)]
    outs = lax.switch(step[0] % levels, branches, grad, heads, place, proj[0], momentum[0])
    return tuple(out[None] for out in (projected, *outs))


def solution(mesh):
    return jax.shard_map(
        program,
        mesh=mesh,
        in_specs=(
            P("replica", None, "tensor"),
            P("replica", "tensor", None),
            P("replica", "tensor", None),
            P("replica", None, None),
            P("replica", None),
            P(),
        ),
        out_specs=(
            P("replica", "tensor", None),
            P("replica", None, "tensor"),
            P("replica", "tensor", None),
            P("replica", "tensor", None),
        ),
        check_vma=False,
    )
```

```python
from functools import partial

import jax
import jax.numpy as jnp
from jax import lax
from jax.experimental import pallas as pl
from jax.experimental.pallas import tpu as pltpu
from jax.sharding import PartitionSpec as P

SEGS = 96
BETA_MOM = 0.9
STEP_RATE = 0.1
NX = 4
ROW = 4
SMALL = pltpu.CompilerParams(vmem_limit_bytes=16 << 20)
SCALARS = pl.BlockSpec(memory_space=pltpu.SMEM)


def vmem(count):
    return [pl.BlockSpec(memory_space=pltpu.VMEM)] * count


def swap_z(x, odd):
    size = lax.axis_size("tensor")
    step = lambda i: -NX if (i // NX + odd) % 2 else NX
    return lax.ppermute(x, "tensor", [(i, (i + step(i)) % size) for i in range(size)])


def exchange_x(x):
    size = lax.axis_size("tensor")
    runs = [list(range(i, i + NX)) for i in range(0, size, NX)]
    return lax.all_to_all(x, "tensor", 0, 0, axis_index_groups=runs, tiled=True)


def pass_replica(x, by):
    size = lax.axis_size("replica")
    return lax.ppermute(x, "replica", [(i, (i + by) % size) for i in range(size)])


def place_of(j, k, z, nz):
    return lax.rem(z + (1 - 2 * lax.rem(z, 2)) * j + nz, nz) * NX + k


def order_kernel(nz, place_ref, rows_ref, out_ref):
    for j in range(nz):
        for k in range(NX):
            out_ref[j * NX + k] = rows_ref[place_of(j, k, place_ref[0], nz)]


def times_rows(heads_ref, blocks, first, held):
    rows = blocks[0].shape[0]
    for j, block in enumerate(blocks):
        held[j * rows : (j + 1) * rows, :] = block
    count = len(blocks) * rows
    return lax.dot_general(
        heads_ref[first * rows : first * rows + count, :],
        held[:count, :],
        (((0,), (0,)), ((), ())),
        preferred_element_type=jnp.float32,
    )


def near_kernel(nz, heads_ref, *refs):
    blocks, out_ref, held, other = refs[:-3], refs[-3], refs[-2], refs[-1]
    low, tile = nz // 2 - 1, held.shape[1]
    for c in range(0, out_ref.shape[1], tile):
        part = [block[:, c : c + tile] for block in blocks]
        out_ref[:, c : c + tile] = times_rows(heads_ref, part[:low], 0, held) + times_rows(
            heads_ref, part[low:], nz // 2 + 2, other
        )


def moment_kernel(scaling, nz, first, heads_ref, *refs):
    blocks, near_ref, mom_ref, out_ref, held = refs[:-4], refs[-4], refs[-3], refs[-2], refs[-1]
    tile = held.shape[1]
    for c in range(0, out_ref.shape[1], tile):
        own, full = slice(c, c + tile), slice(first + c, first + c + tile)
        part = [blocks[0][:, full], blocks[1][:, own], blocks[2][:, full]]
        total = near_ref[:, full] + times_rows(heads_ref, part, nz // 2 - 1, held)
        out_ref[:, own] = (BETA_MOM * mom_ref[:, full].astype(jnp.float32) + total * scaling).astype(
            jnp.bfloat16
        )


def near_of(heads, blocks):
    nz, (rows, width) = len(blocks), blocks[0].shape
    deep = heads.shape[1]
    tile = min(512, width)
    near = [blocks[j] for j in range(nz) if abs(j - nz // 2) > 1]
    return pl.pallas_call(
        partial(near_kernel, nz),
        out_shape=jax.ShapeDtypeStruct((deep, width), jnp.float32),
        in_specs=vmem(1 + len(near)),
        out_specs=vmem(1)[0],
        scratch_shapes=[
            pltpu.VMEM(((nz // 2 - 1) * rows, tile), jnp.bfloat16),
            pltpu.VMEM(((nz // 2 - 2) * rows, tile), jnp.bfloat16),
        ],
        cost_estimate=pl.CostEstimate(
            flops=2 * deep * len(near) * rows * width, bytes_accessed=2 * len(near) * rows * width, transcendentals=0
        ),
        name="near",
        compiler_params=SMALL,
    )(heads, *near)


def moment_of(heads, blocks, near, mom, scaling, part):
    nz, (rows, width) = len(blocks), blocks[0].shape
    deep, cols = heads.shape[1], width // 2
    tile = min(512, cols)
    far = [blocks[nz // 2 - 1], blocks[nz // 2][part], blocks[nz // 2 + 1]]
    return pl.pallas_call(
        partial(moment_kernel, scaling, nz, part * cols),
        out_shape=jax.ShapeDtypeStruct((deep, cols), jnp.bfloat16),
        in_specs=vmem(3 + len(far)),
        out_specs=vmem(1)[0],
        scratch_shapes=[pltpu.VMEM((len(far) * rows, tile), jnp.bfloat16)],
        cost_estimate=pl.CostEstimate(
            flops=2 * deep * len(far) * rows * cols, bytes_accessed=8 * deep * cols, transcendentals=0
        ),
        name="moment",
        compiler_params=SMALL,
    )(heads, *far, near, mom)


def mix_kernel(*refs):
    w_ref, partner_w_ref, moments, new_w_ref, new_m_ref = refs[0], refs[1], refs[2:-2], refs[-2], refs[-1]
    wide = lambda x: x.astype(jnp.float32)
    narrow = lambda x: x.astype(jnp.bfloat16)
    half = moments[0].shape[1]
    for c in range(2):
        part = slice(c * half, (c + 1) * half)
        moment, partner_m = wide(moments[c][...]), wide(moments[2 + c][...])
        updated = narrow(wide(w_ref[:, part]) - STEP_RATE * moment)
        partner_u = narrow(wide(partner_w_ref[:, part]) - STEP_RATE * partner_m)
        new_w_ref[:, part] = narrow((wide(updated) + wide(partner_u)) * 0.5)
        new_m_ref[:, part] = narrow((moment + partner_m) * 0.5)


def back_kernel(scaling, nz, place_ref, *refs):
    w_ref, out_ref = refs[-2], refs[-1]
    rows, half = out_ref.shape[1], w_ref.shape[1] // 2
    times = lambda a, w: lax.dot_general(
        a, w, (((1,), (1,)), ((), ())), preferred_element_type=jnp.float32
    )
    for j in range(nz):
        if j == nz // 2:
            total = times(refs[j][...], w_ref[:, :half]) + times(refs[nz][...], w_ref[:, half:])
        else:
            total = times(refs[j][...], w_ref[...])
        for k in range(NX):
            out_ref[place_of(j, k, place_ref[0], nz)] = (
                total[k * rows : (k + 1) * rows] * scaling
            ).astype(jnp.bfloat16)


def sum_stage(heads_in, weight, target_rows, seg_rows):
    tokens, deep = heads_in.shape
    size = lax.axis_size("tensor")
    nz, rows = size // NX, tokens // size
    chunk = rows * NX
    scaling = (deep * size) ** (-0.5)
    own = lax.axis_index("tensor")
    place = (own // NX).astype(jnp.int32)[None]
    with jax.named_scope("order"):
        heads = pl.pallas_call(
            partial(order_kernel, nz),
            out_shape=jax.ShapeDtypeStruct((size, rows, deep), jnp.bfloat16),
            in_specs=[SCALARS] + vmem(1),
            out_specs=vmem(1)[0],
            name="order",
            compiler_params=SMALL,
        )(place, heads_in.reshape(size, rows, deep)).reshape(tokens, deep)
    first_row = own * rows
    own_seg = lax.dynamic_slice_in_dim(seg_rows, first_row, rows, 0)
    doc_sizes = jnp.sum((own_seg[:, None] == seg_rows[None, :]).astype(jnp.float32), axis=1)
    own_weights = (tokens / (SEGS * doc_sizes))[:, None]
    own_targets = lax.dynamic_slice_in_dim(target_rows, first_row, rows, 0).astype(jnp.float32)

    def share(j):
        j = j % nz
        return scaling * jnp.dot(
            heads[j * chunk : (j + 1) * chunk], weight, preferred_element_type=jnp.float32
        )

    with jax.named_scope("sum_z"):
        half = weight.shape[1] // 2
        term = share(nz // 2).astype(jnp.bfloat16)
        even, odd = swap_z(term[:, :half], 0), swap_z(term[:, half:], 1)
        even = jnp.pad(even.astype(jnp.float32), ((0, 0), (0, half)))
        odd = jnp.pad(odd.astype(jnp.float32), ((0, 0), (half, 0)))
        for m in range(nz // 2 - 1, 0, -1):
            to_even = (share(m) + odd).astype(jnp.bfloat16)
            to_odd = (share(-m) + even).astype(jnp.bfloat16)
            even, odd = swap_z(to_even, 0).astype(jnp.float32), swap_z(to_odd, 1).astype(jnp.float32)
        total = share(0) + even + odd
    with jax.named_scope("sum_x"):
        parts = exchange_x(total.astype(jnp.bfloat16)).reshape(NX, rows, -1)
        mine = jnp.sum(parts.astype(jnp.float32), axis=0)
    grad = ((mine - own_targets) * own_weights).astype(jnp.bfloat16)
    return mine.astype(jnp.bfloat16), grad, heads, place


def update_stage(hop, grad, heads, place, weight, moment_in):
    tokens, deep = heads.shape
    rows, width = grad.shape
    size = lax.axis_size("tensor")
    nz = size // NX
    scaling = (deep * size) ** (-0.5)
    with jax.named_scope("early_partner"):
        half = width // 2
        partner_w = pass_replica(weight, hop)
    with jax.named_scope("gather_x"):
        block = exchange_x(jnp.tile(grad, (NX, 1)))
    with jax.named_scope("gather_z"):
        held = [block] + [None] * (nz - 1)
        even = odd = block
        for m in range(1, nz // 2):
            if hop >= ROW and m == 2:
                odd, partner_w = lax.optimization_barrier((odd, partner_w))
            if hop < ROW and m == 3:
                even, partner_w = lax.optimization_barrier((even, partner_w))
            even, odd = swap_z(odd, 0), swap_z(even, 1)
            held[m], held[-m] = even, odd
        near = near_of(heads, held)
        even = lax.optimization_barrier((near, even))[1]
        odd = lax.optimization_barrier((near, odd))[1]
        held[nz // 2] = (swap_z(even[:, :half], 1), swap_z(odd[:, half:], 0))
    moments, partner_m = [], []
    for c in range(2):
        moments.append(moment_of(heads, held, near, moment_in, scaling, c))
        with jax.named_scope("partner"):
            partner_m.append(pass_replica(moments[c], hop))
    with jax.named_scope("mix"):
        new_w, new_m = pl.pallas_call(
            mix_kernel,
            out_shape=[jax.ShapeDtypeStruct(weight.shape, jnp.bfloat16)] * 2,
            in_specs=vmem(6),
            out_specs=vmem(2),
            name="mix",
            compiler_params=SMALL,
        )(weight, partner_w, *moments, *partner_m)
    with jax.named_scope("back"):
        attn_grad = pl.pallas_call(
            partial(back_kernel, scaling, nz),
            out_shape=jax.ShapeDtypeStruct((size, rows, deep), jnp.bfloat16),
            in_specs=[SCALARS] + vmem(nz + 2),
            out_specs=vmem(1)[0],
            cost_estimate=pl.CostEstimate(
                flops=2 * tokens * width * deep, bytes_accessed=2 * tokens * width, transcendentals=0
            ),
            name="back",
            compiler_params=SMALL,
        )(place, *[h[0] if isinstance(h, tuple) else h for h in held], held[nz // 2][1], weight).reshape(tokens, deep)
    return attn_grad, new_w, new_m


def program(attn_out, proj, momentum, target, segment_ids, step):
    levels = lax.axis_size("replica").bit_length() - 1
    projected, grad, heads, place = sum_stage(attn_out[0], proj[0], target[0], segment_ids[0])
    branches = [partial(update_stage, 1 << bit) for bit in range(levels)]
    outs = lax.switch(step[0] % levels, branches, grad, heads, place, proj[0], momentum[0])
    return tuple(out[None] for out in (projected, *outs))


def solution(mesh):
    return jax.shard_map(
        program,
        mesh=mesh,
        in_specs=(
            P("replica", None, "tensor"),
            P("replica", "tensor", None),
            P("replica", "tensor", None),
            P("replica", None, None),
            P("replica", None),
            P(),
        ),
        out_specs=(
            P("replica", "tensor", None),
            P("replica", None, "tensor"),
            P("replica", "tensor", None),
            P("replica", "tensor", None),
        ),
        check_vma=False,
    )
```

```python
from functools import partial

import jax
import jax.numpy as jnp
from jax import lax
from jax.experimental import pallas as pl
from jax.experimental.pallas import tpu as pltpu
from jax.sharding import PartitionSpec as P

SEGS = 96
BETA_MOM = 0.9
STEP_RATE = 0.1
NX = 4
ROW = 4
SMALL = pltpu.CompilerParams(vmem_limit_bytes=16 << 20)
SCALARS = pl.BlockSpec(memory_space=pltpu.SMEM)


def vmem(count):
    return [pl.BlockSpec(memory_space=pltpu.VMEM)] * count


def swap_z(x, odd):
    size = lax.axis_size("tensor")
    step = lambda i: -NX if (i // NX + odd) % 2 else NX
    return lax.ppermute(x, "tensor", [(i, (i + step(i)) % size) for i in range(size)])


def exchange_x(x):
    size = lax.axis_size("tensor")
    runs = [list(range(i, i + NX)) for i in range(0, size, NX)]
    return lax.all_to_all(x, "tensor", 0, 0, axis_index_groups=runs, tiled=True)


def pass_replica(x, by):
    size = lax.axis_size("replica")
    return lax.ppermute(x, "replica", [(i, (i + by) % size) for i in range(size)])


def place_of(j, k, z, nz):
    return lax.rem(z + (1 - 2 * lax.rem(z, 2)) * j + nz, nz) * NX + k


def order_kernel(nz, place_ref, rows_ref, out_ref):
    for j in range(nz):
        for k in range(NX):
            out_ref[j * NX + k] = rows_ref[place_of(j, k, place_ref[0], nz)]


def times_rows(heads_ref, blocks, first, held):
    rows = blocks[0].shape[0]
    for j, block in enumerate(blocks):
        held[j * rows : (j + 1) * rows, :] = block
    count = len(blocks) * rows
    return lax.dot_general(
        heads_ref[first * rows : first * rows + count, :],
        held[:count, :],
        (((0,), (0,)), ((), ())),
        preferred_element_type=jnp.float32,
    )


def near_kernel(nz, heads_ref, *refs):
    blocks, out_ref, held, other = refs[:-3], refs[-3], refs[-2], refs[-1]
    low, tile = nz // 2 - 1, held.shape[1]

    @pl.loop(0, out_ref.shape[1] // tile)
    def _(i):
        full = pl.ds(pl.multiple_of(i * tile, tile), tile)
        part = [block[:, full] for block in blocks]
        out_ref[:, full] = times_rows(heads_ref, part[:low], 0, held) + times_rows(
            heads_ref, part[low:], nz // 2 + 2, other
        )


def moment_kernel(scaling, nz, first, heads_ref, *refs):
    blocks, near_ref, mom_ref, out_ref, held = refs[:-4], refs[-4], refs[-3], refs[-2], refs[-1]
    tile = held.shape[1]

    @pl.loop(0, out_ref.shape[1] // tile)
    def _(i):
        own = pl.ds(pl.multiple_of(i * tile, tile), tile)
        full = pl.ds(pl.multiple_of(first + i * tile, tile), tile)
        part = [blocks[0][:, full], blocks[1][:, own], blocks[2][:, full]]
        total = near_ref[:, full] + times_rows(heads_ref, part, nz // 2 - 1, held)
        out_ref[:, own] = (BETA_MOM * mom_ref[:, full].astype(jnp.float32) + total * scaling).astype(
            jnp.bfloat16
        )


def near_of(heads, blocks):
    nz, (rows, width) = len(blocks), blocks[0].shape
    deep = heads.shape[1]
    tile = min(512, width)
    near = [blocks[j] for j in range(nz) if abs(j - nz // 2) > 1]
    return pl.pallas_call(
        partial(near_kernel, nz),
        out_shape=jax.ShapeDtypeStruct((deep, width), jnp.float32),
        in_specs=vmem(1 + len(near)),
        out_specs=vmem(1)[0],
        scratch_shapes=[
            pltpu.VMEM(((nz // 2 - 1) * rows, tile), jnp.bfloat16),
            pltpu.VMEM(((nz // 2 - 2) * rows, tile), jnp.bfloat16),
        ],
        cost_estimate=pl.CostEstimate(
            flops=2 * deep * len(near) * rows * width, bytes_accessed=2 * len(near) * rows * width, transcendentals=0
        ),
        name="near",
        compiler_params=SMALL,
    )(heads, *near)


def moment_of(heads, blocks, near, mom, scaling, part):
    nz, (rows, width) = len(blocks), blocks[0].shape
    deep, cols = heads.shape[1], width // 2
    tile = min(512, cols)
    far = [blocks[nz // 2 - 1], blocks[nz // 2][part], blocks[nz // 2 + 1]]
    return pl.pallas_call(
        partial(moment_kernel, scaling, nz, part * cols),
        out_shape=jax.ShapeDtypeStruct((deep, cols), jnp.bfloat16),
        in_specs=vmem(3 + len(far)),
        out_specs=vmem(1)[0],
        scratch_shapes=[pltpu.VMEM((len(far) * rows, tile), jnp.bfloat16)],
        cost_estimate=pl.CostEstimate(
            flops=2 * deep * len(far) * rows * cols, bytes_accessed=8 * deep * cols, transcendentals=0
        ),
        name="moment",
        compiler_params=SMALL,
    )(heads, *far, near, mom)


def mix_kernel(*refs):
    w_ref, partner_w_ref, moments, new_w_ref, new_m_ref = refs[0], refs[1], refs[2:-2], refs[-2], refs[-1]
    wide = lambda x: x.astype(jnp.float32)
    narrow = lambda x: x.astype(jnp.bfloat16)
    half = moments[0].shape[1]

    @pl.loop(0, w_ref.shape[0] // 32)
    def _(i):
        rows = pl.ds(pl.multiple_of(i * 32, 32), 32)
        for c in range(2):
            part = slice(c * half, (c + 1) * half)
            moment, partner_m = wide(moments[c][rows, :]), wide(moments[2 + c][rows, :])
            updated = narrow(wide(w_ref[rows, part]) - STEP_RATE * moment)
            partner_u = narrow(wide(partner_w_ref[rows, part]) - STEP_RATE * partner_m)
            new_w_ref[rows, part] = narrow((wide(updated) + wide(partner_u)) * 0.5)
            new_m_ref[rows, part] = narrow((moment + partner_m) * 0.5)


def back_kernel(scaling, nz, place_ref, *refs):
    w_ref, out_ref = refs[-2], refs[-1]
    rows, half = out_ref.shape[1], w_ref.shape[1] // 2
    times = lambda a, w: lax.dot_general(
        a, w, (((1,), (1,)), ((), ())), preferred_element_type=jnp.float32
    )
    for j in range(nz):
        if j == nz // 2:
            total = times(refs[j][...], w_ref[:, :half]) + times(refs[nz][...], w_ref[:, half:])
        else:
            total = times(refs[j][...], w_ref[...])
        for k in range(NX):
            out_ref[place_of(j, k, place_ref[0], nz)] = (
                total[k * rows : (k + 1) * rows] * scaling
            ).astype(jnp.bfloat16)


def sum_stage(heads_in, weight, target_rows, seg_rows):
    tokens, deep = heads_in.shape
    size = lax.axis_size("tensor")
    nz, rows = size // NX, tokens // size
    chunk = rows * NX
    scaling = (deep * size) ** (-0.5)
    own = lax.axis_index("tensor")
    place = (own // NX).astype(jnp.int32)[None]
    with jax.named_scope("order"):
        heads = pl.pallas_call(
            partial(order_kernel, nz),
            out_shape=jax.ShapeDtypeStruct((size, rows, deep), jnp.bfloat16),
            in_specs=[SCALARS] + vmem(1),
            out_specs=vmem(1)[0],
            name="order",
            compiler_params=SMALL,
        )(place, heads_in.reshape(size, rows, deep)).reshape(tokens, deep)
    first_row = own * rows
    own_seg = lax.dynamic_slice_in_dim(seg_rows, first_row, rows, 0)
    doc_sizes = jnp.sum((own_seg[:, None] == seg_rows[None, :]).astype(jnp.float32), axis=1)
    own_weights = (tokens / (SEGS * doc_sizes))[:, None]
    own_targets = lax.dynamic_slice_in_dim(target_rows, first_row, rows, 0).astype(jnp.float32)

    def share(j):
        j = j % nz
        return scaling * jnp.dot(
            heads[j * chunk : (j + 1) * chunk], weight, preferred_element_type=jnp.float32
        )

    with jax.named_scope("sum_z"):
        half = weight.shape[1] // 2
        term = share(nz // 2).astype(jnp.bfloat16)
        even, odd = swap_z(term[:, :half], 0), swap_z(term[:, half:], 1)
        even = jnp.pad(even.astype(jnp.float32), ((0, 0), (0, half)))
        odd = jnp.pad(odd.astype(jnp.float32), ((0, 0), (half, 0)))
        for m in range(nz // 2 - 1, 0, -1):
            to_even = (share(m) + odd).astype(jnp.bfloat16)
            to_odd = (share(-m) + even).astype(jnp.bfloat16)
            even, odd = swap_z(to_even, 0).astype(jnp.float32), swap_z(to_odd, 1).astype(jnp.float32)
        total = share(0) + even + odd
    with jax.named_scope("sum_x"):
        parts = exchange_x(total.astype(jnp.bfloat16)).reshape(NX, rows, -1)
        mine = jnp.sum(parts.astype(jnp.float32), axis=0)
    grad = ((mine - own_targets) * own_weights).astype(jnp.bfloat16)
    return mine.astype(jnp.bfloat16), grad, heads, place


def update_stage(hop, grad, heads, place, weight, moment_in):
    tokens, deep = heads.shape
    rows, width = grad.shape
    size = lax.axis_size("tensor")
    nz = size // NX
    scaling = (deep * size) ** (-0.5)
    with jax.named_scope("early_partner"):
        half = width // 2
        partner_w = pass_replica(weight, hop)
    with jax.named_scope("gather_x"):
        block = exchange_x(jnp.tile(grad, (NX, 1)))
    with jax.named_scope("gather_z"):
        held = [block] + [None] * (nz - 1)
        even = odd = block
        for m in range(1, nz // 2):
            if hop >= ROW and m == 2:
                odd, partner_w = lax.optimization_barrier((odd, partner_w))
            if hop < ROW and m == 3:
                even, partner_w = lax.optimization_barrier((even, partner_w))
            even, odd = swap_z(odd, 0), swap_z(even, 1)
            held[m], held[-m] = even, odd
        near = near_of(heads, held)
        even = lax.optimization_barrier((near, even))[1]
        odd = lax.optimization_barrier((near, odd))[1]
        held[nz // 2] = (swap_z(even[:, :half], 1), swap_z(odd[:, half:], 0))
    moments, partner_m = [], []
    for c in range(2):
        moments.append(moment_of(heads, held, near, moment_in, scaling, c))
        with jax.named_scope("partner"):
            partner_m.append(pass_replica(moments[c], hop))
    with jax.named_scope("mix"):
        new_w, new_m = pl.pallas_call(
            mix_kernel,
            out_shape=[jax.ShapeDtypeStruct(weight.shape, jnp.bfloat16)] * 2,
            in_specs=vmem(6),
            out_specs=vmem(2),
            name="mix",
            compiler_params=SMALL,
        )(weight, partner_w, *moments, *partner_m)
    with jax.named_scope("back"):
        attn_grad = pl.pallas_call(
            partial(back_kernel, scaling, nz),
            out_shape=jax.ShapeDtypeStruct((size, rows, deep), jnp.bfloat16),
            in_specs=[SCALARS] + vmem(nz + 2),
            out_specs=vmem(1)[0],
            cost_estimate=pl.CostEstimate(
                flops=2 * tokens * width * deep, bytes_accessed=2 * tokens * width, transcendentals=0
            ),
            name="back",
            compiler_params=SMALL,
        )(place, *[h[0] if isinstance(h, tuple) else h for h in held], held[nz // 2][1], weight).reshape(tokens, deep)
    return attn_grad, new_w, new_m


def program(attn_out, proj, momentum, target, segment_ids, step):
    levels = lax.axis_size("replica").bit_length() - 1
    projected, grad, heads, place = sum_stage(attn_out[0], proj[0], target[0], segment_ids[0])
    branches = [partial(update_stage, 1 << bit) for bit in range(levels)]
    outs = lax.switch(step[0] % levels, branches, grad, heads, place, proj[0], momentum[0])
    return tuple(out[None] for out in (projected, *outs))


def solution(mesh):
    return jax.shard_map(
        program,
        mesh=mesh,
        in_specs=(
            P("replica", None, "tensor"),
            P("replica", "tensor", None),
            P("replica", "tensor", None),
            P("replica", None, None),
            P("replica", None),
            P(),
        ),
        out_specs=(
            P("replica", "tensor", None),
            P("replica", None, "tensor"),
            P("replica", "tensor", None),
            P("replica", "tensor", None),
        ),
        check_vma=False,
    )
```

```python
from functools import partial

import jax
import jax.numpy as jnp
from jax import lax
from jax.experimental import pallas as pl
from jax.experimental.pallas import tpu as pltpu
from jax.sharding import PartitionSpec as P

SEGS = 96
BETA_MOM = 0.9
STEP_RATE = 0.1
NX = 4
ROW = 4
SMALL = pltpu.CompilerParams(vmem_limit_bytes=16 << 20)
SCALARS = pl.BlockSpec(memory_space=pltpu.SMEM)


def vmem(count):
    return [pl.BlockSpec(memory_space=pltpu.VMEM)] * count


def swap_z(x, odd):
    size = lax.axis_size("tensor")
    step = lambda i: -NX if (i // NX + odd) % 2 else NX
    return lax.ppermute(x, "tensor", [(i, (i + step(i)) % size) for i in range(size)])


def exchange_x(x):
    size = lax.axis_size("tensor")
    runs = [list(range(i, i + NX)) for i in range(0, size, NX)]
    return lax.all_to_all(x, "tensor", 0, 0, axis_index_groups=runs, tiled=True)


def pass_replica(x, by):
    size = lax.axis_size("replica")
    return lax.ppermute(x, "replica", [(i, (i + by) % size) for i in range(size)])


def place_of(j, k, z, nz):
    return lax.rem(z + (1 - 2 * lax.rem(z, 2)) * j + nz, nz) * NX + k


def order_kernel(nz, place_ref, rows_ref, out_ref):
    for j in range(nz):
        for k in range(NX):
            out_ref[j * NX + k] = rows_ref[place_of(j, k, place_ref[0], nz)]


def times_rows(heads_ref, blocks, first, held):
    rows = blocks[0].shape[0]
    for j, block in enumerate(blocks):
        held[j * rows : (j + 1) * rows, :] = block
    count = len(blocks) * rows
    return lax.dot_general(
        heads_ref[first * rows : first * rows + count, :],
        held[:count, :],
        (((0,), (0,)), ((), ())),
        preferred_element_type=jnp.float32,
    )


def near_kernel(nz, heads_ref, *refs):
    blocks, out_ref, held, other = refs[:-3], refs[-3], refs[-2], refs[-1]
    low, tile = nz // 2 - 1, held.shape[1]

    @pl.loop(0, out_ref.shape[1] // tile)
    def _(i):
        full = pl.ds(pl.multiple_of(i * tile, tile), tile)
        part = [block[:, full] for block in blocks]
        out_ref[:, full] = times_rows(heads_ref, part[:low], 0, held) + times_rows(
            heads_ref, part[low:], nz // 2 + 2, other
        )


def moment_kernel(scaling, nz, first, heads_ref, *refs):
    blocks, near_ref, mom_ref, out_ref, held = refs[:-4], refs[-4], refs[-3], refs[-2], refs[-1]
    tile = held.shape[1]

    @pl.loop(0, out_ref.shape[1] // tile)
    def _(i):
        own = pl.ds(pl.multiple_of(i * tile, tile), tile)
        full = pl.ds(pl.multiple_of(first + i * tile, tile), tile)
        part = [blocks[0][:, full], blocks[1][:, own], blocks[2][:, full]]
        total = near_ref[:, full] + times_rows(heads_ref, part, nz // 2 - 1, held)
        out_ref[:, own] = (BETA_MOM * mom_ref[:, full].astype(jnp.float32) + total * scaling).astype(
            jnp.bfloat16
        )


def near_of(heads, blocks):
    nz, (rows, width) = len(blocks), blocks[0].shape
    deep = heads.shape[1]
    tile = min(512, width)
    near = [blocks[j] for j in range(nz) if abs(j - nz // 2) > 1]
    return pl.pallas_call(
        partial(near_kernel, nz),
        out_shape=jax.ShapeDtypeStruct((deep, width), jnp.float32),
        in_specs=vmem(1 + len(near)),
        out_specs=vmem(1)[0],
        scratch_shapes=[
            pltpu.VMEM(((nz // 2 - 1) * rows, tile), jnp.bfloat16),
            pltpu.VMEM(((nz // 2 - 2) * rows, tile), jnp.bfloat16),
        ],
        cost_estimate=pl.CostEstimate(
            flops=2 * deep * len(near) * rows * width, bytes_accessed=2 * len(near) * rows * width, transcendentals=0
        ),
        name="near",
        compiler_params=SMALL,
    )(heads, *near)


def moment_of(heads, blocks, near, mom, scaling, part):
    nz, (rows, width) = len(blocks), blocks[0].shape
    deep, cols = heads.shape[1], width // 2
    tile = min(512, cols)
    far = [blocks[nz // 2 - 1], blocks[nz // 2][part], blocks[nz // 2 + 1]]
    return pl.pallas_call(
        partial(moment_kernel, scaling, nz, part * cols),
        out_shape=jax.ShapeDtypeStruct((deep, cols), jnp.bfloat16),
        in_specs=vmem(3 + len(far)),
        out_specs=vmem(1)[0],
        scratch_shapes=[pltpu.VMEM((len(far) * rows, tile), jnp.bfloat16)],
        cost_estimate=pl.CostEstimate(
            flops=2 * deep * len(far) * rows * cols, bytes_accessed=8 * deep * cols, transcendentals=0
        ),
        name="moment",
        compiler_params=SMALL,
    )(heads, *far, near, mom)


def mix_kernel(*refs):
    w_ref, partner_w_ref, moments, new_w_ref, new_m_ref = refs[0], refs[1], refs[2:-2], refs[-2], refs[-1]
    wide = lambda x: x.astype(jnp.float32)
    narrow = lambda x: x.astype(jnp.bfloat16)
    half = moments[0].shape[1]

    @pl.loop(0, w_ref.shape[0] // 32)
    def _(i):
        rows = pl.ds(pl.multiple_of(i * 32, 32), 32)
        for c in range(2):
            part = slice(c * half, (c + 1) * half)
            moment, partner_m = wide(moments[c][rows, :]), wide(moments[2 + c][rows, :])
            updated = narrow(wide(w_ref[rows, part]) - STEP_RATE * moment)
            partner_u = narrow(wide(partner_w_ref[rows, part]) - STEP_RATE * partner_m)
            new_w_ref[rows, part] = narrow((wide(updated) + wide(partner_u)) * 0.5)
            new_m_ref[rows, part] = narrow((moment + partner_m) * 0.5)


def back_kernel(scaling, nz, place_ref, *refs):
    w_ref, out_ref = refs[-2], refs[-1]
    rows, half = out_ref.shape[1], w_ref.shape[1] // 2
    times = lambda a, w: lax.dot_general(
        a, w, (((1,), (1,)), ((), ())), preferred_element_type=jnp.float32
    )
    for j in range(nz):
        if j == nz // 2:
            total = times(refs[j][...], w_ref[:, :half]) + times(refs[nz][...], w_ref[:, half:])
        else:
            total = times(refs[j][...], w_ref[...])
        for k in range(NX):
            out_ref[place_of(j, k, place_ref[0], nz)] = (
                total[k * rows : (k + 1) * rows] * scaling
            ).astype(jnp.bfloat16)


def grad_kernel(parts_ref, target_ref, weights_ref, sum_ref, grads_ref):
    total = parts_ref[0].astype(jnp.float32)
    for k in range(1, NX):
        total = total + parts_ref[k].astype(jnp.float32)
    sum_ref[...] = total.astype(jnp.bfloat16)
    grad = ((total - target_ref[...].astype(jnp.float32)) * weights_ref[...]).astype(jnp.bfloat16)
    for k in range(NX):
        grads_ref[k] = grad


def sum_stage(heads_in, weight, target_rows, seg_rows):
    tokens, deep = heads_in.shape
    size = lax.axis_size("tensor")
    nz, rows = size // NX, tokens // size
    chunk = rows * NX
    scaling = (deep * size) ** (-0.5)
    own = lax.axis_index("tensor")
    place = (own // NX).astype(jnp.int32)[None]
    with jax.named_scope("order"):
        heads = pl.pallas_call(
            partial(order_kernel, nz),
            out_shape=jax.ShapeDtypeStruct((size, rows, deep), jnp.bfloat16),
            in_specs=[SCALARS] + vmem(1),
            out_specs=vmem(1)[0],
            name="order",
            compiler_params=SMALL,
        )(place, heads_in.reshape(size, rows, deep)).reshape(tokens, deep)
    first_row = own * rows
    own_seg = lax.dynamic_slice_in_dim(seg_rows, first_row, rows, 0)
    doc_sizes = jnp.sum((own_seg[:, None] == seg_rows[None, :]).astype(jnp.float32), axis=1)
    own_weights = (tokens / (SEGS * doc_sizes))[:, None]
    own_targets = lax.dynamic_slice_in_dim(target_rows, first_row, rows, 0)

    def share(j):
        j = j % nz
        return scaling * jnp.dot(
            heads[j * chunk : (j + 1) * chunk], weight, preferred_element_type=jnp.float32
        )

    with jax.named_scope("sum_z"):
        half = weight.shape[1] // 2
        term = share(nz // 2).astype(jnp.bfloat16)
        even, odd = swap_z(term[:, :half], 0), swap_z(term[:, half:], 1)
        even = jnp.pad(even.astype(jnp.float32), ((0, 0), (0, half)))
        odd = jnp.pad(odd.astype(jnp.float32), ((0, 0), (half, 0)))
        for m in range(nz // 2 - 1, 0, -1):
            to_even = (share(m) + odd).astype(jnp.bfloat16)
            to_odd = (share(-m) + even).astype(jnp.bfloat16)
            even, odd = swap_z(to_even, 0).astype(jnp.float32), swap_z(to_odd, 1).astype(jnp.float32)
        total = share(0) + even + odd
    with jax.named_scope("sum_x"):
        parts = exchange_x(total.astype(jnp.bfloat16)).reshape(NX, rows, -1)
    width = weight.shape[1]
    with jax.named_scope("grad"):
        sums, grads = pl.pallas_call(
            grad_kernel,
            out_shape=[
                jax.ShapeDtypeStruct((rows, width), jnp.bfloat16),
                jax.ShapeDtypeStruct((NX, rows, width), jnp.bfloat16),
            ],
            in_specs=vmem(3),
            out_specs=vmem(2),
            name="grad",
            compiler_params=SMALL,
        )(parts, own_targets, own_weights)
    return sums, grads.reshape(NX * rows, width), heads, place


def update_stage(hop, grads, heads, place, weight, moment_in):
    tokens, deep = heads.shape
    rows, width = grads.shape[0] // NX, grads.shape[1]
    size = lax.axis_size("tensor")
    nz = size // NX
    scaling = (deep * size) ** (-0.5)
    with jax.named_scope("early_partner"):
        half = width // 2
        partner_w = pass_replica(weight, hop)
    with jax.named_scope("gather_x"):
        block = exchange_x(grads)
    with jax.named_scope("gather_z"):
        held = [block] + [None] * (nz - 1)
        even = odd = block
        for m in range(1, nz // 2):
            if hop >= ROW and m == 2:
                odd, partner_w = lax.optimization_barrier((odd, partner_w))
            if hop < ROW and m == 3:
                even, partner_w = lax.optimization_barrier((even, partner_w))
            even, odd = swap_z(odd, 0), swap_z(even, 1)
            held[m], held[-m] = even, odd
        near = near_of(heads, held)
        even = lax.optimization_barrier((near, even))[1]
        odd = lax.optimization_barrier((near, odd))[1]
        held[nz // 2] = (swap_z(even[:, :half], 1), swap_z(odd[:, half:], 0))
    moments, partner_m = [], []
    for c in range(2):
        moments.append(moment_of(heads, held, near, moment_in, scaling, c))
        with jax.named_scope("partner"):
            partner_m.append(pass_replica(moments[c], hop))
    with jax.named_scope("mix"):
        new_w, new_m = pl.pallas_call(
            mix_kernel,
            out_shape=[jax.ShapeDtypeStruct(weight.shape, jnp.bfloat16)] * 2,
            in_specs=vmem(6),
            out_specs=vmem(2),
            name="mix",
            compiler_params=SMALL,
        )(weight, partner_w, *moments, *partner_m)
    with jax.named_scope("back"):
        attn_grad = pl.pallas_call(
            partial(back_kernel, scaling, nz),
            out_shape=jax.ShapeDtypeStruct((size, rows, deep), jnp.bfloat16),
            in_specs=[SCALARS] + vmem(nz + 2),
            out_specs=vmem(1)[0],
            cost_estimate=pl.CostEstimate(
                flops=2 * tokens * width * deep, bytes_accessed=2 * tokens * width, transcendentals=0
            ),
            name="back",
            compiler_params=SMALL,
        )(place, *[h[0] if isinstance(h, tuple) else h for h in held], held[nz // 2][1], weight).reshape(tokens, deep)
    return attn_grad, new_w, new_m


def program(attn_out, proj, momentum, target, segment_ids, step):
    levels = lax.axis_size("replica").bit_length() - 1
    projected, grads, heads, place = sum_stage(attn_out[0], proj[0], target[0], segment_ids[0])
    branches = [partial(update_stage, 1 << bit) for bit in range(levels)]
    outs = lax.switch(step[0] % levels, branches, grads, heads, place, proj[0], momentum[0])
    return tuple(out[None] for out in (projected, *outs))


def solution(mesh):
    return jax.shard_map(
        program,
        mesh=mesh,
        in_specs=(
            P("replica", None, "tensor"),
            P("replica", "tensor", None),
            P("replica", "tensor", None),
            P("replica", None, None),
            P("replica", None),
            P(),
        ),
        out_specs=(
            P("replica", "tensor", None),
            P("replica", None, "tensor"),
            P("replica", "tensor", None),
            P("replica", "tensor", None),
        ),
        check_vma=False,
    )
```
